32 devices in a mesh: chan: 8 (over y, x, core), tm: 4 (over z).
Axes of the slice: x: 2, y: 2, z: 4, core: 2. Of those that a mesh axis runs over, the one named last changes fastest.
Arguments:
- record: bfloat16 [20480, 8192], P('chan', 'tm'), may hold values from -6 to 6
- fir_taps: bfloat16 [129], replicated, may hold values from -0.5 to 0.5
- space_taps: float32 [9], replicated, may hold values from -2 to 2
- range_probe: bfloat16 [8192, 128], P('tm'), may hold values from -0.0625 to 0.0625
- corange_probe: bfloat16 [20480, 256], P('chan'), may hold values from -0.0625 to 0.0625
Outputs:
- range_sketch: float32 [20480, 128], P(('chan', 'tm'))
- corange_sketch: float32 [256, 8192], P('chan', 'tm')
The draws below stay inside these ranges and needn't reach their ends.
All inputs are finite; a program needn't handle non-finite values.
Results may differ from the reference program's by a relative error of at most 0.0041.
Values may be sent and summed in bfloat16 or wider, within the bound.
No kernel may reach another device: no remote copies, remote signals or barrier semaphores. Data moves between devices by JAX's collectives and lax.ppermute only.
A program may use at most 192 MiB of HBM per device.

```python
import jax
import jax.numpy as jnp
from jax import lax

C_DEV = 2560
TAPS = 129
CHTAPS = 9
SKETCH = 128
CORANGE = 256
CH = 20480
TS = 8192
N_CHAN = 8


def strengthened(result, key, source, target, parts, factor):
    def block_of(position):
        return (jnp.arange(result.shape[position]) // (result.shape[position] // parts)).reshape((-1,) + (1,) * (result.ndim - 1 - position))

    near = jax.random.permutation(key, parts)[block_of(target)]
    far = (block_of(target) + parts // 2) % parts
    return jnp.where((block_of(source) == near) | (block_of(source) == far), factor * result, result)


def block_scale(stream_key, extent, pieces, smallest, largest):
    loudness, own = 1.0, jax.random.fold_in(stream_key, 6)
    for position, parts in pieces:
        heights = jnp.exp(jax.random.uniform(jax.random.fold_in(own, position), (parts,), jnp.float32, smallest / len(pieces), largest / len(pieces)))
        loudness = loudness * jnp.repeat(heights, extent[position] // parts).reshape([-1 if axis == position else 1 for axis in range(len(extent))])
    return loudness


def normal_values(own_key, dims, width, reach, pieces=(), held_as=jnp.bfloat16):
    gain = block_scale(own_key, dims, pieces, -0.22, 0.18) if pieces else 1.0
    drawn = jax.random.normal(own_key, dims, jnp.float32) * width * gain
    return jnp.minimum(jnp.maximum(drawn, -reach), reach).astype(held_as)


def gaussian_with(own_key, dims, spread, bound, shards, heavy, kind=jnp.bfloat16):
    values = spread * jax.random.normal(own_key, dims, jnp.float32)
    if shards:
        values = values * block_scale(own_key, dims, shards, -0.22, 0.18)
    return jnp.clip(strengthened(values, jax.random.fold_in(own_key, 3), *heavy), -bound, bound).astype(kind)


def setup_inputs(seed: int = 0) -> dict:
    seeds = jax.random.split(jax.random.key(seed), 6)
    return {
        "record": normal_values(seeds[0], (CH, TS), 1.0, 6.0, ((0, 8), (1, 4))),
        "fir_taps": normal_values(seeds[1], (TAPS,), TAPS ** -0.5, 0.5),
        "space_taps": normal_values(seeds[2], (CHTAPS,), CHTAPS ** -0.5, 2.0, (), jnp.float32),
        "range_probe": normal_values(seeds[3], (TS, SKETCH), TS ** -0.5, 0.0625, ((0, 4),)),
        "corange_probe": gaussian_with(seeds[4], (CH, CORANGE), CH ** -0.5, 0.0625, ((0, 8),), (0, 1, 8, 2.0)),
    }


def toeplitz(fir_taps):
    extended = jnp.concatenate([fir_taps, jnp.zeros((128,), fir_taps.dtype)])
    tiled = jnp.tile(extended, 128)[:128 * 256].reshape(128, 256)
    return tiled.T


def fir_block(record_block, band_matrix):
    channels = record_block.shape[0]
    padded = jnp.pad(record_block, ((0, 0), (64, 64)))
    low_part = padded[:, :TS].reshape(-1, 128)
    high_part = padded[:, 128:TS + 128].reshape(-1, 128)
    summed = jnp.dot(low_part, band_matrix[:128], preferred_element_type=jnp.float32)
    summed = summed + jnp.dot(high_part, band_matrix[128:], preferred_element_type=jnp.float32)
    return summed.reshape(channels, TS).astype(jnp.bfloat16)


def reference(record, fir_taps, space_taps, range_probe, corange_probe):
    band_matrix = toeplitz(fir_taps)
    blocks = record.reshape(N_CHAN, C_DEV, TS)
    filtered = lax.map(lambda record_block: fir_block(record_block, band_matrix), blocks).reshape(CH, TS)
    padded = jnp.pad(filtered, ((4, 4), (0, 0)))

    def advance(running, block_index):
        first_row = (block_index * C_DEV).astype(jnp.int32)
        window = lax.dynamic_slice_in_dim(padded, first_row, C_DEV + 8, 0)
        summed = jnp.zeros((C_DEV, TS), jnp.float32)
        for offset in range(CHTAPS):
            summed = summed + space_taps[offset] * window[offset:offset + C_DEV].astype(jnp.float32)
        mixed_field = summed.astype(jnp.bfloat16)
        sketch_rows = jnp.dot(mixed_field, range_probe, preferred_element_type=jnp.float32)
        probe_block = lax.dynamic_slice_in_dim(corange_probe, first_row, C_DEV, 0)
        partial_value = lax.dot_general(probe_block, mixed_field, (((0,), (0,)), ((), ())), preferred_element_type=jnp.float32)
        return running + partial_value, sketch_rows

    running, sketch_rows = lax.scan(advance, jnp.zeros((CORANGE, TS), jnp.float32), jnp.arange(N_CHAN, dtype=jnp.int32))
    return sketch_rows.reshape(CH, SKETCH), running
```

```python
import functools

import jax
import jax.numpy as jnp
from jax import lax
from jax.experimental import pallas as pl
from jax.experimental.pallas import tpu as pltpu
from jax.sharding import PartitionSpec as P

TAPS = 129
HALF = 64
CHTAPS = 9
EDGE = 8
F32 = jnp.float32
BF16 = jnp.bfloat16
NT = (((1,), (1,)), ((), ()))
VMEM_LIMIT = 56 << 20

whole = functools.partial(pl.BlockSpec, memory_space=pltpu.VMEM)
smem = functools.partial(pl.BlockSpec, memory_space=pltpu.SMEM)


def split(value):
    high = value.astype(BF16)
    return high, (value - high.astype(F32)).astype(BF16)


def diagonals(row, rows, lanes, shift):
    spread = jnp.broadcast_to(row, (rows, lanes))
    return pltpu.roll(spread, shift % lanes, 1, stride=1, stride_axis=0)


def range_kernel(count, record, row_a, row_b, probe, probe_a, probe_b, taps, *rest):
    outs, (padded, probes, total) = rest[:count], rest[count:]
    step = pl.program_id(0)
    rows, samples = record.shape
    width = probe.shape[1]
    channels = total.shape[0] - 2 * EDGE
    tm, chan = lax.axis_index("tm"), lax.axis_index("chan")

    @pl.when(step == 0)
    def _():
        spread = diagonals(taps[...], 256, 512, -128)[:, :128]
        band = spread.T.astype(BF16)
        odd = lax.rem(tm, 2)
        padded[HALF : HALF + samples, :] = probe[...]
        padded[pl.ds(pl.multiple_of((1 - odd) * (HALF + samples), HALF), HALF), :] = probe_a[...]
        padded[pl.ds(pl.multiple_of(odd * (HALF + samples), HALF), HALF), :] = probe_b[...]
        for block in range(samples // 128):
            filtered = jnp.dot(
                band, padded[128 * block : 128 * block + 256, :], preferred_element_type=F32
            )
            high, low = split(filtered)
            probes[128 * block : 128 * block + 128, :width] = high
            probes[128 * block : 128 * block + 128, width:] = low
        odd = lax.rem(chan, 2)
        edges = jnp.concatenate([row_a[...], row_b[...]], axis=0)
        pair = jnp.dot(edges, probes[...], preferred_element_type=F32)
        sums = pair[:, :width] + pair[:, width:]
        total[pl.ds(pl.multiple_of((1 - odd) * (EDGE + channels), EDGE), EDGE), :] = sums[:EDGE]
        total[pl.ds(pl.multiple_of(odd * (EDGE + channels), EDGE), EDGE), :] = sums[EDGE:]

    pair = jnp.dot(record[...], probes[...], preferred_element_type=F32)
    total[pl.ds(pl.multiple_of(EDGE + step * rows, EDGE), rows), :] = pair[:, :width] + pair[:, width:]

    @pl.when(step == pl.num_programs(0) - 1)
    def _():
        share = channels // count
        for distance in range(count):
            owner = lax.bitwise_xor(tm, distance)
            start = pl.multiple_of(owner * share, EDGE)
            outs[distance][...] = total[pl.ds(start, share + 2 * EDGE), :].astype(
                outs[distance].dtype
            )


def range_partials(record, row_a, row_b, probe, probe_a, probe_b, taps, count):
    channels, samples = record.shape
    width = probe.shape[1]
    rows = channels // 5
    share = channels // count + 2 * EDGE
    return pl.pallas_call(
        functools.partial(range_kernel, count),
        grid=(channels // rows,),
        in_specs=[pl.BlockSpec((rows, samples), lambda i: (i, 0))] + [whole()] * 6,
        out_specs=[whole()] * count,
        out_shape=[
            jax.ShapeDtypeStruct((share, width), F32 if distance == 0 else BF16)
            for distance in range(count)
        ],
        scratch_shapes=[
            pltpu.VMEM((samples + 2 * HALF, width), BF16),
            pltpu.VMEM((samples, 2 * width), BF16),
            pltpu.VMEM((channels + 2 * EDGE, width), F32),
        ],
        compiler_params=pltpu.CompilerParams(vmem_limit_bytes=VMEM_LIMIT),
        cost_estimate=pl.CostEstimate(
            flops=4 * channels * samples * width,
            bytes_accessed=2 * channels * samples,
            transcendentals=0,
        ),
        name="range_partials",
    )(record, row_a, row_b, probe, probe_a, probe_b, taps)


def corange_kernel(
    count, record, row_a, row_b, probe, taps, space, other, mine, padded, filtered, rim, acc, pairs, full
):
    step = pl.program_id(0)
    rows, samples = record.shape
    channels, width = probe.shape
    chan = lax.axis_index("chan")
    odd = lax.rem(chan, 2)

    @pl.when(step == 0)
    def _():
        lane = lax.broadcasted_iota(jnp.int32, (1, 256), 1)
        row = jnp.zeros((1, 256), F32)
        for tap in range(CHTAPS):
            row = jnp.where(lane == tap + 188, space[tap], row)
        band = diagonals(row, 256, 256, 0)[:, :128].T
        bands = jnp.concatenate(list(split(band)), axis=0)
        padded[:192, :] = jnp.zeros((192, width), BF16)
        padded[192 : 192 + channels, :] = probe[...]
        padded[192 + channels :, :] = jnp.zeros((192, width), BF16)

        def block_of(block):
            both = jnp.dot(
                bands, padded[128 * block : 128 * block + 256, :], preferred_element_type=F32
            )
            return (both[:128] + both[128:]).T.astype(BF16)

        last = channels // 128 + 1
        for block in range(1, last):
            filtered[:, 128 * block - 128 : 128 * block] = block_of(block)
        lanes = lax.broadcasted_iota(jnp.int32, (width, 128), 1)
        ends = jnp.where(lanes < 64, block_of(last).astype(F32), block_of(0).astype(F32)).astype(BF16)
        rim[...] = jnp.zeros_like(rim)
        rim[pl.ds(pl.multiple_of(odd * (128 - EDGE), EDGE), EDGE), :] = row_a[...].astype(F32)
        rim[pl.ds(pl.multiple_of((1 - odd) * (128 - EDGE), EDGE), EDGE), :] = row_b[...].astype(F32)
        acc[...] = jnp.dot(ends, rim[...].astype(BF16), preferred_element_type=F32)

    part = filtered[:, pl.ds(pl.multiple_of(step * rows, 128), rows)]
    acc[...] += jnp.dot(part, record[...], preferred_element_type=F32)

    @pl.when(step == pl.num_programs(0) - 1)
    def _():
        band = diagonals(pltpu.roll(jnp.broadcast_to(taps[...], (8, 512)), HALF, 1)[:1], 256, 512, 0).astype(BF16)
        pairs[:, :128] = jnp.zeros((2 * width, 128), BF16)
        pairs[:, 128 + samples :] = jnp.zeros((2 * width, 128), BF16)
        high, low = split(acc[...])
        pairs[:width, 128 : 128 + samples] = high
        pairs[width:, 128 : 128 + samples] = low
        for block in range(samples // 256):
            both = lax.dot_general(
                pairs[:, 256 * block : 256 * block + 512], band, NT, preferred_element_type=F32
            )
            full[:, 256 * block : 256 * block + 256] = both[:width] + both[width:]
        both = lax.dot_general(
            pairs[:, 128:256], band[:128, 256:384], NT, preferred_element_type=F32
        )
        both = both + lax.dot_general(
            pairs[:, samples : 128 + samples], band[:128, :128], NT, preferred_element_type=F32
        )
        full[:, samples:] = both[:width] + both[width:]
        share = width // count
        chip = lax.div(chan, 2)
        for distance in range(count // 2):
            base = 2 * lax.bitwise_xor(chip, distance)
            keep = pl.multiple_of((base + odd) * share, share)
            give = pl.multiple_of((base + 1 - odd) * share, share)
            mine[distance] = full[pl.ds(keep, share), :]
            other[distance] = full[pl.ds(give, share), :].astype(BF16)


def corange_partials(record, row_a, row_b, probe, taps, space, count):
    channels, samples = record.shape
    width = probe.shape[1]
    rows = channels // 5
    shape = (count // 2, width // count, samples + 128)
    return pl.pallas_call(
        functools.partial(corange_kernel, count),
        grid=(channels // rows,),
        in_specs=[pl.BlockSpec((rows, samples), lambda i: (i, 0))] + [whole()] * 4 + [smem()],
        out_specs=[whole()] * 2,
        out_shape=[jax.ShapeDtypeStruct(shape, BF16), jax.ShapeDtypeStruct(shape, F32)],
        scratch_shapes=[
            pltpu.VMEM((channels + 384, width), BF16),
            pltpu.VMEM((width, channels), BF16),
            pltpu.VMEM((128, samples), F32),
            pltpu.VMEM((width, samples), F32),
            pltpu.VMEM((2 * width, samples + 256), BF16),
            pltpu.VMEM((width, samples + 128), F32),
        ],
        compiler_params=pltpu.CompilerParams(vmem_limit_bytes=VMEM_LIMIT),
        cost_estimate=pl.CostEstimate(
            flops=2 * channels * samples * width,
            bytes_accessed=2 * channels * samples,
            transcendentals=0,
        ),
        name="corange_partials",
    )(record, row_a, row_b, probe, taps, space)


def pair_sum_kernel(mine, got, *outs):
    for distance, out in enumerate(outs):
        out[...] = (mine[distance] + got[distance].astype(F32)).astype(out.dtype)


def pair_sum(mine, got):
    count, share, length = mine.shape
    return pl.pallas_call(
        pair_sum_kernel,
        in_specs=[whole()] * 2,
        out_specs=[whole()] * count,
        out_shape=[
            jax.ShapeDtypeStruct((share, length), F32 if distance == 0 else BF16)
            for distance in range(count)
        ],
        compiler_params=pltpu.CompilerParams(vmem_limit_bytes=VMEM_LIMIT),
        name="pair_sum",
    )(mine, got)


def corange_sum_kernel(*refs):
    parts, main, edge = refs[:-2], refs[-2], refs[-1]
    samples = main.shape[1]
    value = parts[0][...]
    for part in parts[1:]:
        value = value + part[...].astype(F32)
    main[...] = value[:, :samples]
    edge[...] = value[:, samples:]


def corange_sum(parts):
    share, length = parts[0].shape
    return pl.pallas_call(
        corange_sum_kernel,
        in_specs=[whole()] * len(parts),
        out_specs=[whole()] * 2,
        out_shape=[
            jax.ShapeDtypeStruct((share, length - 128), F32),
            jax.ShapeDtypeStruct((share, 128), F32),
        ],
        compiler_params=pltpu.CompilerParams(vmem_limit_bytes=VMEM_LIMIT),
        name="corange_sum",
    )(*parts)


def corange_edges_kernel(main, edge_a, edge_b, out):
    odd = lax.rem(lax.axis_index("tm"), 2)
    samples = main.shape[1]
    lane = lax.broadcasted_iota(jnp.int32, edge_a.shape, 1)
    before = jnp.where(odd == 1, edge_a[...], edge_b[...])
    after = jnp.where(odd == 1, edge_b[...], edge_a[...])
    out[...] = main[...]
    out[:, :128] = main[:, :128] + jnp.where(lane < HALF, before, 0.0)
    out[:, samples - 128 :] = main[:, samples - 128 :] + jnp.where(lane >= HALF, after, 0.0)


def corange_edges(main, edge_a, edge_b):
    return pl.pallas_call(
        corange_edges_kernel,
        in_specs=[whole()] * 3,
        out_specs=whole(),
        out_shape=jax.ShapeDtypeStruct(main.shape, F32),
        name="corange_edges",
    )(main, edge_a, edge_b)


def range_sum_kernel(space, *refs):
    parts, out, total = refs[:-2], refs[-2], refs[-1]
    value = parts[0][...]
    for part in parts[1:]:
        value = value + part[...].astype(F32)
    total[...] = value
    share = out.shape[0]
    result = space[0] * total[4 : 4 + share, :]
    for tap in range(1, CHTAPS):
        result = result + space[tap] * total[4 + tap : 4 + tap + share, :]
    out[...] = result


def range_sum(space, parts):
    rows, width = parts[0].shape
    return pl.pallas_call(
        range_sum_kernel,
        in_specs=[smem()] + [whole()] * len(parts),
        out_specs=whole(),
        out_shape=jax.ShapeDtypeStruct((rows - 2 * EDGE, width), F32),
        scratch_shapes=[pltpu.VMEM((rows, width), F32)],
        name="range_sum",
    )(space, *parts)


def swaps(first, second, axis):
    count = lax.axis_size(axis)
    low = [(i, i ^ 1) for i in range(count)]
    high = [(i, i + 1) for i in range(1, count - 1, 2)]
    high = high + [(target, source) for source, target in high]
    return lax.ppermute(first, axis, low), lax.ppermute(second, axis, high)


def ends(block, width, axis):
    even = lax.axis_index(axis) % 2 == 0
    low, high = block[:width], block[-width:]
    return jnp.where(even, high, low), jnp.where(even, low, high)


def on_device(record, fir_taps, space_taps, range_probe, corange_probe):
    n_tm, n_chan = lax.axis_size("tm"), lax.axis_size("chan")
    taps = jnp.pad(fir_taps.astype(F32), (0, 512 - TAPS)).reshape(1, 512)
    row_a, row_b = swaps(*ends(record, EDGE, "chan"), "chan")
    probe_a, probe_b = swaps(*ends(range_probe, HALF, "tm"), "tm")
    shares = range_partials(record, row_a, row_b, range_probe, probe_a, probe_b, taps, n_tm)
    got = [shares[0]]
    for distance in range(n_tm - 1, 0, -1):
        pairs = [(i, i ^ distance) for i in range(n_tm)]
        got.append(lax.ppermute(shares[distance], "tm", pairs))
    other, mine = corange_partials(record, row_a, row_b, corange_probe, taps, space_taps, n_chan)
    other = lax.ppermute(other, "chan", [(i, i ^ 1) for i in range(n_chan)])
    sums = pair_sum(mine, other)
    parts = [sums[0]]
    for distance in range(n_chan // 2 - 1, 0, -1):
        pairs = [(i, i ^ (2 * distance)) for i in range(n_chan)]
        parts.append(lax.ppermute(sums[distance], "chan", pairs))
    main, edge = corange_sum(parts)
    corange_sketch = corange_edges(main, *swaps(edge, edge, "tm"))
    range_sketch = range_sum(space_taps, got)
    return (range_sketch, corange_sketch)


def solution(mesh):
    return jax.shard_map(
        on_device,
        mesh=mesh,
        in_specs=(P("chan", "tm"), P(), P(), P("tm", None), P("chan", None)),
        out_specs=(P(("chan", "tm"), None), P("chan", "tm")),
        check_vma=False,
    )
```

```python
import functools

import jax
import jax.numpy as jnp
from jax import lax
from jax.experimental import pallas as pl
from jax.experimental.pallas import tpu as pltpu
from jax.sharding import PartitionSpec as P

TAPS = 129
HALF = 64
CHTAPS = 9
EDGE = 8
CHUNKS = 5
F32 = jnp.float32
BF16 = jnp.bfloat16
NT = (((1,), (1,)), ((), ()))
VMEM_LIMIT = 24 << 20

whole = functools.partial(pl.BlockSpec, memory_space=pltpu.VMEM)
smem = functools.partial(pl.BlockSpec, memory_space=pltpu.SMEM)
anywhere = functools.partial(pl.BlockSpec, memory_space=pl.ANY)
params = pltpu.CompilerParams(vmem_limit_bytes=VMEM_LIMIT)


def near(value):
    return pltpu.with_memory_space_constraint(value, pltpu.VMEM)


def split(value):
    high = value.astype(BF16)
    return high, (value - high.astype(F32)).astype(BF16)


def diagonals(row, rows, lanes, shift):
    spread = jnp.broadcast_to(row, (rows, lanes))
    return pltpu.roll(spread, shift % lanes, 1, stride=1, stride_axis=0)


def far(value):
    return pltpu.with_memory_space_constraint(value, pltpu.HBM)


def quick():
    return pl.CostEstimate(flops=0, bytes_accessed=0, transcendentals=0)


def taps_row(fir):
    taps = fir[...].astype(F32).reshape(1, TAPS)
    return jnp.concatenate([taps, jnp.zeros((1, 512 - TAPS), F32)], axis=1)


def range_part(give, keep, record, row_a, row_b, probe, probe_a, probe_b, fir, padded, probes, total):
    channels, samples = record.shape
    width = probe.shape[1]
    tm, chan = lax.axis_index("tm"), lax.axis_index("chan")
    count = lax.axis_size("tm")
    lead = diagonals(taps_row(fir), 256, 512, -128)[:, :128].T.astype(BF16)
    odd = lax.rem(chan, 2)
    padded[HALF : HALF + samples, :] = probe[...]
    padded[pl.ds(pl.multiple_of(odd * (HALF + samples), HALF), HALF), :] = probe_a[...]
    padded[pl.ds(pl.multiple_of((1 - odd) * (HALF + samples), HALF), HALF), :] = probe_b[...]
    for block in range(samples // 128):
        high, low = split(
            jnp.dot(lead, padded[128 * block : 128 * block + 256, :], preferred_element_type=F32)
        )
        probes[128 * block : 128 * block + 128, :width] = high
        probes[128 * block : 128 * block + 128, width:] = low
    edges = jnp.concatenate([row_a[...], row_b[...]], axis=0)
    pair = jnp.dot(edges, probes[...], preferred_element_type=F32)
    sums = pair[:, :width] + pair[:, width:]
    total[pl.ds(pl.multiple_of((1 - odd) * (EDGE + channels), EDGE), EDGE), :] = sums[:EDGE]
    total[pl.ds(pl.multiple_of(odd * (EDGE + channels), EDGE), EDGE), :] = sums[EDGE:]
    rows = channels // CHUNKS
    @pl.loop(0, CHUNKS)
    def _(step):
        start = pl.multiple_of(step * rows, 16)
        pair = jnp.dot(record[pl.ds(start, rows), :], probes[...], preferred_element_type=F32)
        total[pl.ds(pl.multiple_of(start + EDGE, EDGE), rows), :] = pair[:, :width] + pair[:, width:]

    share = channels // count
    for target, first in ((give, lax.bitwise_xor(tm, 1)), (keep, tm)):
        for index in range(count // 2):
            start = pl.multiple_of(lax.bitwise_xor(first, 2 * index) * share, EDGE)
            target[index] = total[pl.ds(start, share + 2 * EDGE), :].astype(target.dtype)


def corange_part(other, mine, record, row_a, row_b, probe, fir, space, padded, filtered, rim, pairs, full):
    channels, samples = record.shape
    width = probe.shape[1]
    count = lax.axis_size("chan")
    late = pltpu.roll(jnp.broadcast_to(taps_row(fir), (8, 512)), HALF, 1)[:1]
    band = diagonals(late, 256, 512, 0).astype(BF16)
    lane = lax.broadcasted_iota(jnp.int32, (1, 256), 1)
    row = jnp.zeros((1, 256), F32)
    for tap in range(CHTAPS):
        row = jnp.where(lane == tap + 188, space[tap], row)
    both = jnp.concatenate(list(split(diagonals(row, 256, 256, 0)[:, :128].T)), axis=0)
    padded[:192, :] = jnp.zeros((192, width), BF16)
    padded[192 : 192 + channels, :] = probe[...]
    padded[192 + channels :, :] = jnp.zeros((192, width), BF16)

    def block_of(block):
        pair = jnp.dot(both, padded[128 * block : 128 * block + 256, :], preferred_element_type=F32)
        return (pair[:128] + pair[128:]).T

    last = channels // 128 + 1
    for block in range(1, last):
        filtered[:, 128 * block - 128 : 128 * block] = block_of(block).astype(BF16)
    lanes = lax.broadcasted_iota(jnp.int32, (width, 128), 1)
    ends = jnp.where(lanes < 64, block_of(last), block_of(0)).astype(BF16)
    chan = lax.axis_index("chan")
    odd = lax.rem(chan, 2)
    rim[...] = jnp.zeros_like(rim)
    rim[pl.ds(pl.multiple_of(odd * (128 - EDGE), EDGE), EDGE), :] = row_a[...].astype(F32)
    rim[pl.ds(pl.multiple_of((1 - odd) * (128 - EDGE), EDGE), EDGE), :] = row_b[...].astype(F32)
    pairs[:, :128] = jnp.zeros((2 * width, 128), BF16)
    pairs[:, 128 + samples :] = jnp.zeros((2 * width, 128), BF16)
    for block in range(0, samples, 512):
        value = jnp.dot(filtered[...], record[:, block : block + 512], preferred_element_type=F32)
        value = value + jnp.dot(
            ends, rim[:, block : block + 512].astype(BF16), preferred_element_type=F32
        )
        high, low = split(value)
        pairs[:width, 128 + block : 640 + block] = high
        pairs[width:, 128 + block : 640 + block] = low
    for block in range(samples // 256):
        pair = lax.dot_general(
            pairs[:, 256 * block : 256 * block + 512], band, NT, preferred_element_type=F32
        )
        full[:, 256 * block : 256 * block + 256] = pair[:width] + pair[width:]
    pair = lax.dot_general(pairs[:, 128:256], band[:128, 256:384], NT, preferred_element_type=F32)
    pair = pair + lax.dot_general(
        pairs[:, samples : 128 + samples], band[:128, :128], NT, preferred_element_type=F32
    )
    full[:, samples:] = pair[:width] + pair[width:]
    share = width // count
    chip = lax.div(chan, 2)
    for distance in range(count // 2):
        base = 2 * lax.bitwise_xor(chip, distance)
        keep = pl.multiple_of((base + odd) * share, share)
        give = pl.multiple_of((base + 1 - odd) * share, share)
        mine[distance] = full[pl.ds(keep, share), :]
        other[distance] = full[pl.ds(give, share), :].astype(BF16)


def partials_kernel(
    record, row_a, row_b, range_probe, probe_a, probe_b, corange_source, fir, space, other, mine, give, keep,
    corange_probe, sem, *scratch,
):
    copy = pltpu.make_async_copy(corange_source, corange_probe, sem)
    copy.start()
    range_part(give, keep, record, row_a, row_b, range_probe, probe_a, probe_b, fir, *scratch[:3])
    copy.wait()
    corange_part(other, mine, record, row_a, row_b, corange_probe, fir, space, *scratch[3:])


def partials(record, row_a, row_b, range_probe, probe_a, probe_b, corange_probe, fir, space):
    n_tm, n_chan = lax.axis_size("tm"), lax.axis_size("chan")
    channels, samples = record.shape
    sketch, corange = range_probe.shape[1], corange_probe.shape[1]
    shape = (n_chan // 2, corange // n_chan, samples + 128)
    shares = (n_tm // 2, channels // n_tm + 2 * EDGE, sketch)
    return pl.pallas_call(
        partials_kernel,
        in_specs=[whole()] * 6 + [anywhere(), whole(), smem()],
        out_specs=[whole()] * 4,
        out_shape=[
            pltpu.VMEM(shape, BF16),
            pltpu.VMEM(shape, F32),
            pltpu.VMEM(shares, BF16),
            pltpu.VMEM(shares, F32),
        ],
        scratch_shapes=[
            pltpu.VMEM(corange_probe.shape, BF16),
            pltpu.SemaphoreType.DMA,
            pltpu.VMEM((samples + 2 * HALF, sketch), BF16),
            pltpu.VMEM((samples, 2 * sketch), BF16),
            pltpu.VMEM((channels + 2 * EDGE, sketch), F32),
            pltpu.VMEM((channels + 384, corange), BF16),
            pltpu.VMEM((corange, channels), BF16),
            pltpu.VMEM((128, samples), F32),
            pltpu.VMEM((2 * corange, samples + 256), BF16),
            pltpu.VMEM((corange, samples + 128), F32),
        ],
        compiler_params=pltpu.CompilerParams(vmem_limit_bytes=30 << 20),
        cost_estimate=quick(),
        name="partials",
    )(
        near(record), near(row_a), near(row_b), near(range_probe), near(probe_a), near(probe_b),
        far(corange_probe), fir, far(space),
    )


def halve_kernel(held, got, after, give, keep):
    for index in range(keep.shape[0]):
        keep[index] = held[2 * index] + got[2 * index].astype(F32)
        give[index] = (held[2 * index + 1] + got[2 * index + 1].astype(F32)).astype(BF16)


def halve(held, got, after):
    shape = (held.shape[0] // 2, *held.shape[1:])
    return pl.pallas_call(
        halve_kernel,
        in_specs=[whole()] * 2 + [anywhere()],
        out_specs=[whole()] * 2,
        out_shape=[pltpu.VMEM(shape, BF16), pltpu.VMEM(shape, F32)],
        compiler_params=params,
        cost_estimate=quick(),
        name="halve",
    )(held, near(got), after)


def range_exchange(give, keep, after):
    count, distance = lax.axis_size("tm"), 1
    while True:
        got = lax.ppermute(give, "tm", [(i, i ^ distance) for i in range(count)])
        distance *= 2
        if distance == count:
            return keep, got
        give, keep = halve(keep, got, after)


def pair_sum_kernel(mine, got, *outs):
    for distance, out in enumerate(outs):
        out[...] = (mine[distance] + got[distance].astype(F32)).astype(out.dtype)


def pair_sum(mine, got):
    count, share, length = mine.shape
    return pl.pallas_call(
        pair_sum_kernel,
        in_specs=[whole()] * 2,
        out_specs=[whole()] * count,
        out_shape=[
            pltpu.VMEM((share, length), F32 if distance == 0 else BF16) for distance in range(count)
        ],
        compiler_params=params,
        cost_estimate=quick(),
        name="pair_sum",
    )(mine, near(got))


def corange_sum_kernel(*refs):
    parts, main, edge = refs[:-2], refs[-2], refs[-1]
    samples = main.shape[1]
    value = parts[0][...]
    for part in parts[1:]:
        value = value + part[...].astype(F32)
    main[...] = value[:, :samples]
    edge[...] = value[:, samples:]


def corange_sum(parts):
    share, length = parts[0].shape
    return pl.pallas_call(
        corange_sum_kernel,
        in_specs=[whole()] * len(parts),
        out_specs=[whole()] * 2,
        out_shape=[
            pltpu.VMEM((share, length - 128), F32),
            pltpu.VMEM((share, 128), F32),
        ],
        compiler_params=params,
        cost_estimate=quick(),
        name="corange_sum",
    )(*[near(part) for part in parts])


def corange_edges_kernel(main, edge_a, edge_b, out):
    odd = lax.rem(lax.axis_index("tm"), 2)
    samples = main.shape[1]
    lane = lax.broadcasted_iota(jnp.int32, edge_a.shape, 1)
    before = jnp.where(odd == 1, edge_a[...], edge_b[...])
    after = jnp.where(odd == 1, edge_b[...], edge_a[...])
    out[...] = main[...]
    out[:, :128] = main[:, :128] + jnp.where(lane < HALF, before, 0.0)
    out[:, samples - 128 :] = main[:, samples - 128 :] + jnp.where(lane >= HALF, after, 0.0)


def corange_edges(main, edge_a, edge_b):
    return pl.pallas_call(
        corange_edges_kernel,
        in_specs=[whole()] * 3,
        out_specs=whole(),
        out_shape=jax.ShapeDtypeStruct(main.shape, F32),
        compiler_params=params,
        cost_estimate=quick(),
        name="corange_edges",
    )(main, near(edge_a), near(edge_b))


def range_sum_kernel(space, *refs):
    parts, out, total = refs[:-2], refs[-2], refs[-1]
    value = parts[0][0] + parts[1][0].astype(F32)
    rows, width = value.shape
    high, low = split(value)
    total[:rows, :width] = high
    total[:rows, width:] = low
    total[rows:, :] = jnp.zeros((total.shape[0] - rows, 2 * width), BF16)
    lane = lax.broadcasted_iota(jnp.int32, (1, 128), 1)
    row = jnp.zeros((1, 128), F32)
    for tap in range(CHTAPS):
        row = jnp.where(lane == tap + 4, space[tap], row)
    band = jnp.concatenate(list(split(diagonals(row, 64, 128, 0))), axis=0)
    for start in range(0, out.shape[0], 64):
        pair = jnp.dot(band, total[start : start + 128, :], preferred_element_type=F32)
        pair = pair[:64] + pair[64:]
        out[start : start + 64, :] = pair[:, :width] + pair[:, width:]


def range_sum(space, parts):
    _, rows, width = parts[0].shape
    return pl.pallas_call(
        range_sum_kernel,
        in_specs=[smem()] + [whole()] * len(parts),
        out_specs=whole(),
        out_shape=jax.ShapeDtypeStruct((rows - 2 * EDGE, width), F32),
        scratch_shapes=[pltpu.VMEM((rows - 2 * EDGE + 64, 2 * width), BF16)],
        compiler_params=params,
        cost_estimate=quick(),
        name="range_sum",
    )(far(space), *[near(part) for part in parts])


def swaps(first, second, axis):
    count = lax.axis_size(axis)
    low = [(i, i ^ 1) for i in range(count)]
    high = [(i, i + 1) for i in range(1, count - 1, 2)]
    high = high + [(target, source) for source, target in high]
    return lax.ppermute(first, axis, low), lax.ppermute(second, axis, high)


def pick_kernel(record, probe, row_a, row_b, probe_a, sems):
    odd = lax.rem(lax.axis_index("chan"), 2)
    far_row, far_probe = record.shape[0] - EDGE, probe.shape[0] - HALF
    copies = [
        pltpu.make_async_copy(source.at[pl.ds(pl.multiple_of(start, size), size)], target, sems.at[slot])
        for slot, (source, start, size, target) in enumerate(
            [
                (record, (1 - odd) * far_row, EDGE, row_a),
                (record, odd * far_row, EDGE, row_b),
                (probe, (1 - odd) * far_probe, HALF, probe_a),
            ]
        )
    ]
    for copy in copies:
        copy.start()
    for copy in copies:
        copy.wait()


def pick(record, probe):
    rows = pltpu.VMEM((EDGE, record.shape[1]), BF16)
    return pl.pallas_call(
        pick_kernel,
        in_specs=[anywhere()] * 2,
        out_specs=[whole()] * 3,
        out_shape=[rows, rows, pltpu.VMEM((HALF, probe.shape[1]), BF16)],
        scratch_shapes=[pltpu.SemaphoreType.DMA((3,))],
        compiler_params=params,
        cost_estimate=pl.CostEstimate(flops=0, bytes_accessed=4 * record.size, transcendentals=0),
        name="pick",
    )(far(record), far(probe))


def probe_ends(edge):
    n_tm, n_chan = lax.axis_size("tm"), lax.axis_size("chan")
    pairs = []
    for chan in range(n_chan):
        for tm in range(n_tm - 1):
            low, high = chan * n_tm + tm, chan * n_tm + tm + 1
            pairs.append((low, high) if chan % 2 == 0 else (high, low))
    got = lax.ppermute(edge, ("chan", "tm"), pairs)
    return got, lax.ppermute(got, "chan", [(i, i ^ 1) for i in range(n_chan)])


def on_device(record, fir_taps, space_taps, range_probe, corange_probe):
    n_chan = lax.axis_size("chan")
    row_a, row_b, edge = pick(record, range_probe)
    probe_a, probe_b = probe_ends(edge)
    row_a, row_b = swaps(row_a, row_b, "chan")
    fir = far(fir_taps)
    other, mine, give, keep = partials(
        record, row_a, row_b, range_probe, probe_a, probe_b, corange_probe, fir, space_taps
    )
    other = lax.ppermute(other, "chan", [(i, i ^ 1) for i in range(n_chan)])
    sums = pair_sum(mine, other)
    parts = [sums[0]]
    for distance in range(1, n_chan // 2):
        pairs = [(i, i ^ (2 * distance)) for i in range(n_chan)]
        parts.append(lax.ppermute(sums[distance], "chan", pairs))
    main, edge = corange_sum(parts)
    got = range_exchange(give, keep, main)
    corange_sketch = corange_edges(main, *swaps(edge, edge, "tm"))
    range_sketch = range_sum(space_taps, got)
    return (range_sketch, corange_sketch)


def solution(mesh):
    return jax.shard_map(
        on_device,
        mesh=mesh,
        in_specs=(P("chan", "tm"), P(), P(), P("tm", None), P("chan", None)),
        out_specs=(P(("chan", "tm"), None), P("chan", "tm")),
        check_vma=False,
    )
```

```python
import functools

import jax
import jax.numpy as jnp
from jax import lax
from jax.experimental import pallas as pl
from jax.experimental.pallas import tpu as pltpu
from jax.sharding import PartitionSpec as P

TAPS = 129
HALF = 64
CHTAPS = 9
EDGE = 8
CHUNKS = 5
F32 = jnp.float32
BF16 = jnp.bfloat16
NT = (((1,), (1,)), ((), ()))
VMEM_LIMIT = 24 << 20

whole = functools.partial(pl.BlockSpec, memory_space=pltpu.VMEM)
smem = functools.partial(pl.BlockSpec, memory_space=pltpu.SMEM)
anywhere = functools.partial(pl.BlockSpec, memory_space=pl.ANY)
params = pltpu.CompilerParams(vmem_limit_bytes=VMEM_LIMIT)


def near(value):
    return pltpu.with_memory_space_constraint(value, pltpu.VMEM)


def split(value):
    high = value.astype(BF16)
    return high, (value - high.astype(F32)).astype(BF16)


def diagonals(row, rows, lanes, shift):
    spread = jnp.broadcast_to(row, (rows, lanes))
    return pltpu.roll(spread, shift % lanes, 1, stride=1, stride_axis=0)


def far(value):
    return pltpu.with_memory_space_constraint(value, pltpu.HBM)


def quick():
    return pl.CostEstimate(flops=0, bytes_accessed=0, transcendentals=0)


def taps_row(fir):
    taps = fir[...].astype(F32).reshape(1, TAPS)
    return jnp.concatenate([taps, jnp.zeros((1, 512 - TAPS), F32)], axis=1)


def prepare_kernel(source, fir, space, filtered, ends, lead, band, last_band, probe, padded, sem):
    channels, width = probe.shape
    copy = pltpu.make_async_copy(source, probe, sem)
    copy.start()
    taps = taps_row(fir)
    lead[...] = diagonals(taps, 256, 512, -128)[:, :128].T.astype(BF16)
    late = pltpu.roll(jnp.broadcast_to(taps, (8, 512)), HALF, 1)[:1]
    band[...] = diagonals(late, 256, 512, 0).astype(BF16)
    lane = lax.broadcasted_iota(jnp.int32, (1, 256), 1)
    row = jnp.zeros((1, 256), F32)
    last_row = jnp.zeros((1, 256), F32)
    for tap in range(CHTAPS):
        row = jnp.where(lane == tap + 188, space[tap], row)
        last_row = jnp.where(lane == tap + 4, space[tap], last_row)
    last_band[...] = jnp.concatenate(list(split(diagonals(last_row[:, :128], 64, 128, 0))), axis=0)
    both = jnp.concatenate(list(split(diagonals(row, 256, 256, 0)[:, :128].T)), axis=0)
    padded[:192, :] = jnp.zeros((192, width), BF16)
    padded[192 + channels :, :] = jnp.zeros((192, width), BF16)
    copy.wait()
    padded[192 : 192 + channels, :] = probe[...]

    def block_of(block):
        pair = jnp.dot(both, padded[128 * block : 128 * block + 256, :], preferred_element_type=F32)
        return (pair[:128] + pair[128:]).T

    last = channels // 128 + 1
    for block in range(1, last):
        filtered[:, 128 * block - 128 : 128 * block] = block_of(block).astype(BF16)
    lanes = lax.broadcasted_iota(jnp.int32, (width, 128), 1)
    ends[...] = jnp.where(lanes < 64, block_of(last), block_of(0)).astype(BF16)


def prepare(probe, fir, space):
    channels, width = probe.shape
    return pl.pallas_call(
        prepare_kernel,
        in_specs=[anywhere(), whole(), smem()],
        out_specs=[whole()] * 5,
        out_shape=[
            pltpu.VMEM((width, channels), BF16),
            pltpu.VMEM((width, 128), BF16),
            pltpu.VMEM((128, 256), BF16),
            pltpu.VMEM((256, 512), BF16),
            pltpu.VMEM((128, 128), BF16),
        ],
        scratch_shapes=[
            pltpu.VMEM(probe.shape, BF16),
            pltpu.VMEM((channels + 384, width), BF16),
            pltpu.SemaphoreType.DMA,
        ],
        compiler_params=params,
        cost_estimate=pl.CostEstimate(flops=0, bytes_accessed=8 << 20, transcendentals=0),
        name="prepare",
    )(far(probe), fir, far(space))


def range_part(give, keep, record, row_a, row_b, probe, probe_a, probe_b, lead, padded, probes, total):
    channels, samples = record.shape
    width = probe.shape[1]
    tm, chan = lax.axis_index("tm"), lax.axis_index("chan")
    count = lax.axis_size("tm")
    odd = lax.rem(chan, 2)
    padded[HALF : HALF + samples, :] = probe[...]
    padded[pl.ds(pl.multiple_of(odd * (HALF + samples), HALF), HALF), :] = probe_a[...]
    padded[pl.ds(pl.multiple_of((1 - odd) * (HALF + samples), HALF), HALF), :] = probe_b[...]
    for block in range(samples // 128):
        high, low = split(
            jnp.dot(lead[...], padded[128 * block : 128 * block + 256, :], preferred_element_type=F32)
        )
        probes[128 * block : 128 * block + 128, :width] = high
        probes[128 * block : 128 * block + 128, width:] = low
    edges = jnp.concatenate([row_a[...], row_b[...]], axis=0)
    pair = jnp.dot(edges, probes[...], preferred_element_type=F32)
    sums = pair[:, :width] + pair[:, width:]
    total[pl.ds(pl.multiple_of((1 - odd) * (EDGE + channels), EDGE), EDGE), :] = sums[:EDGE]
    total[pl.ds(pl.multiple_of(odd * (EDGE + channels), EDGE), EDGE), :] = sums[EDGE:]
    rows = channels // CHUNKS
    for start in range(0, channels, rows):
        pair = jnp.dot(record[start : start + rows, :], probes[...], preferred_element_type=F32)
        total[EDGE + start : EDGE + start + rows, :] = pair[:, :width] + pair[:, width:]

    share = channels // count
    for target, first in ((give, lax.bitwise_xor(tm, 1)), (keep, tm)):
        for index in range(count // 2):
            start = pl.multiple_of(lax.bitwise_xor(first, 2 * index) * share, EDGE)
            target[index] = total[pl.ds(start, share + 2 * EDGE), :].astype(target.dtype)


def corange_part(other, mine, record, row_a, row_b, filtered, ends, band, rim, pairs, full):
    channels, samples = record.shape
    width = filtered.shape[0]
    count = lax.axis_size("chan")
    chan = lax.axis_index("chan")
    odd = lax.rem(chan, 2)
    rim[...] = jnp.zeros_like(rim)
    rim[pl.ds(pl.multiple_of(odd * (128 - EDGE), EDGE), EDGE), :] = row_a[...].astype(F32)
    rim[pl.ds(pl.multiple_of((1 - odd) * (128 - EDGE), EDGE), EDGE), :] = row_b[...].astype(F32)
    pairs[:, :128] = jnp.zeros((2 * width, 128), BF16)
    pairs[:, 128 + samples :] = jnp.zeros((2 * width, 128), BF16)
    for block in range(0, samples, 512):
        value = jnp.dot(filtered[...], record[:, block : block + 512], preferred_element_type=F32)
        value = value + jnp.dot(
            ends[...], rim[:, block : block + 512].astype(BF16), preferred_element_type=F32
        )
        high, low = split(value)
        pairs[:width, 128 + block : 640 + block] = high
        pairs[width:, 128 + block : 640 + block] = low
    for block in range(samples // 256):
        pair = lax.dot_general(
            pairs[:, 256 * block : 256 * block + 512], band[...], NT, preferred_element_type=F32
        )
        full[:, 256 * block : 256 * block + 256] = pair[:width] + pair[width:]
    pair = lax.dot_general(pairs[:, 128:256], band[:128, 256:384], NT, preferred_element_type=F32)
    pair = pair + lax.dot_general(
        pairs[:, samples : 128 + samples], band[:128, :128], NT, preferred_element_type=F32
    )
    full[:, samples:] = pair[:width] + pair[width:]
    share = width // count
    chip = lax.div(chan, 2)
    for distance in range(count // 2):
        base = 2 * lax.bitwise_xor(chip, distance)
        keep = pl.multiple_of((base + odd) * share, share)
        give = pl.multiple_of((base + 1 - odd) * share, share)
        mine[distance] = full[pl.ds(keep, share), :]
        other[distance] = full[pl.ds(give, share), :].astype(BF16)


def partials_kernel(
    record, row_a, row_b, range_probe, probe_a, probe_b, filtered, ends, lead, band, other, mine, give, keep, *scratch
):
    range_part(give, keep, record, row_a, row_b, range_probe, probe_a, probe_b, lead, *scratch[:3])
    corange_part(other, mine, record, row_a, row_b, filtered, ends, band, *scratch[3:])


def partials(record, row_a, row_b, range_probe, probe_a, probe_b, filtered, ends, lead, band):
    n_tm, n_chan = lax.axis_size("tm"), lax.axis_size("chan")
    channels, samples = record.shape
    sketch, corange = range_probe.shape[1], filtered.shape[0]
    shape = (n_chan // 2, corange // n_chan, samples + 128)
    shares = (n_tm // 2, channels // n_tm + 2 * EDGE, sketch)
    return pl.pallas_call(
        partials_kernel,
        in_specs=[whole()] * 10,
        out_specs=[whole()] * 4,
        out_shape=[
            pltpu.VMEM(shape, BF16),
            pltpu.VMEM(shape, F32),
            pltpu.VMEM(shares, BF16),
            pltpu.VMEM(shares, F32),
        ],
        scratch_shapes=[
            pltpu.VMEM((samples + 2 * HALF, sketch), BF16),
            pltpu.VMEM((samples, 2 * sketch), BF16),
            pltpu.VMEM((channels + 2 * EDGE, sketch), F32),
            pltpu.VMEM((128, samples), F32),
            pltpu.VMEM((2 * corange, samples + 256), BF16),
            pltpu.VMEM((corange, samples + 128), F32),
        ],
        compiler_params=params,
        cost_estimate=quick(),
        name="partials",
    )(
        near(record), near(row_a), near(row_b), near(range_probe), near(probe_a), near(probe_b),
        filtered, ends, lead, band,
    )


def halve_kernel(held, got, after, give, keep):
    for index in range(keep.shape[0]):
        keep[index] = held[2 * index] + got[2 * index].astype(F32)
        give[index] = (held[2 * index + 1] + got[2 * index + 1].astype(F32)).astype(BF16)


def halve(held, got, after):
    shape = (held.shape[0] // 2, *held.shape[1:])
    return pl.pallas_call(
        halve_kernel,
        in_specs=[whole()] * 2 + [anywhere()],
        out_specs=[whole()] * 2,
        out_shape=[pltpu.VMEM(shape, BF16), pltpu.VMEM(shape, F32)],
        compiler_params=params,
        cost_estimate=quick(),
        name="halve",
    )(held, near(got), after)


def range_exchange(give, keep, after):
    count, distance = lax.axis_size("tm"), 1
    while True:
        got = lax.ppermute(give, "tm", [(i, i ^ distance) for i in range(count)])
        distance *= 2
        if distance == count:
            return keep, got
        give, keep = halve(keep, got, after)


def pair_sum_kernel(mine, got, *outs):
    for distance, out in enumerate(outs):
        out[...] = (mine[distance] + got[distance].astype(F32)).astype(out.dtype)


def pair_sum(mine, got):
    count, share, length = mine.shape
    return pl.pallas_call(
        pair_sum_kernel,
        in_specs=[whole()] * 2,
        out_specs=[whole()] * count,
        out_shape=[
            pltpu.VMEM((share, length), F32 if distance == 0 else BF16) for distance in range(count)
        ],
        compiler_params=params,
        cost_estimate=quick(),
        name="pair_sum",
    )(mine, near(got))


def corange_sum_kernel(*refs):
    parts, main, edge = refs[:-2], refs[-2], refs[-1]
    samples = main.shape[1]
    value = parts[0][...]
    for part in parts[1:]:
        value = value + part[...].astype(F32)
    main[...] = value[:, :samples]
    edge[...] = value[:, samples:]


def corange_sum(parts):
    share, length = parts[0].shape
    return pl.pallas_call(
        corange_sum_kernel,
        in_specs=[whole()] * len(parts),
        out_specs=[whole()] * 2,
        out_shape=[
            pltpu.VMEM((share, length - 128), F32),
            pltpu.VMEM((share, 128), F32),
        ],
        compiler_params=params,
        cost_estimate=quick(),
        name="corange_sum",
    )(*[near(part) for part in parts])


def corange_edges_kernel(main, edge_a, edge_b, out):
    odd = lax.rem(lax.axis_index("tm"), 2)
    samples = main.shape[1]
    lane = lax.broadcasted_iota(jnp.int32, edge_a.shape, 1)
    before = jnp.where(odd == 1, edge_a[...], edge_b[...])
    after = jnp.where(odd == 1, edge_b[...], edge_a[...])
    out[...] = main[...]
    out[:, :128] = main[:, :128] + jnp.where(lane < HALF, before, 0.0)
    out[:, samples - 128 :] = main[:, samples - 128 :] + jnp.where(lane >= HALF, after, 0.0)


def corange_edges(main, edge_a, edge_b):
    return pl.pallas_call(
        corange_edges_kernel,
        in_specs=[whole()] * 3,
        out_specs=whole(),
        out_shape=jax.ShapeDtypeStruct(main.shape, F32),
        compiler_params=params,
        cost_estimate=quick(),
        name="corange_edges",
    )(main, near(edge_a), near(edge_b))


def range_sum_kernel(band, *refs):
    parts, out, total = refs[:-2], refs[-2], refs[-1]
    value = parts[0][0] + parts[1][0].astype(F32)
    rows, width = value.shape
    high, low = split(value)
    total[:rows, :width] = high
    total[:rows, width:] = low
    total[rows:, :] = jnp.zeros((total.shape[0] - rows, 2 * width), BF16)
    for start in range(0, out.shape[0], 64):
        pair = jnp.dot(band[...], total[start : start + 128, :], preferred_element_type=F32)
        pair = pair[:64] + pair[64:]
        out[start : start + 64, :] = pair[:, :width] + pair[:, width:]


def range_sum(band, parts):
    _, rows, width = parts[0].shape
    return pl.pallas_call(
        range_sum_kernel,
        in_specs=[whole()] * (1 + len(parts)),
        out_specs=whole(),
        out_shape=jax.ShapeDtypeStruct((rows - 2 * EDGE, width), F32),
        scratch_shapes=[pltpu.VMEM((rows - 2 * EDGE + 64, 2 * width), BF16)],
        compiler_params=params,
        cost_estimate=quick(),
        name="range_sum",
    )(band, *[near(part) for part in parts])


def swaps(first, second, axis):
    count = lax.axis_size(axis)
    low = [(i, i ^ 1) for i in range(count)]
    high = [(i, i + 1) for i in range(1, count - 1, 2)]
    high = high + [(target, source) for source, target in high]
    return lax.ppermute(first, axis, low), lax.ppermute(second, axis, high)


def pick_kernel(record, probe, row_a, row_b, probe_a, sems):
    odd = lax.rem(lax.axis_index("chan"), 2)
    far_row, far_probe = record.shape[0] - EDGE, probe.shape[0] - HALF
    copies = [
        pltpu.make_async_copy(source.at[pl.ds(pl.multiple_of(start, size), size)], target, sems.at[slot])
        for slot, (source, start, size, target) in enumerate(
            [
                (record, (1 - odd) * far_row, EDGE, row_a),
                (record, odd * far_row, EDGE, row_b),
                (probe, (1 - odd) * far_probe, HALF, probe_a),
            ]
        )
    ]
    for copy in copies:
        copy.start()
    for copy in copies:
        copy.wait()


def pick(record, probe):
    rows = pltpu.VMEM((EDGE, record.shape[1]), BF16)
    return pl.pallas_call(
        pick_kernel,
        in_specs=[anywhere()] * 2,
        out_specs=[whole()] * 3,
        out_shape=[rows, rows, pltpu.VMEM((HALF, probe.shape[1]), BF16)],
        scratch_shapes=[pltpu.SemaphoreType.DMA((3,))],
        compiler_params=params,
        cost_estimate=pl.CostEstimate(flops=0, bytes_accessed=4 * record.size, transcendentals=0),
        name="pick",
    )(far(record), far(probe))


def probe_ends(edge):
    n_tm, n_chan = lax.axis_size("tm"), lax.axis_size("chan")
    pairs = []
    for chan in range(n_chan):
        for tm in range(n_tm - 1):
            low, high = chan * n_tm + tm, chan * n_tm + tm + 1
            pairs.append((low, high) if chan % 2 == 0 else (high, low))
    got = lax.ppermute(edge, ("chan", "tm"), pairs)
    return got, lax.ppermute(got, "chan", [(i, i ^ 1) for i in range(n_chan)])


def on_device(record, fir_taps, space_taps, range_probe, corange_probe):
    n_chan = lax.axis_size("chan")
    row_a, row_b, edge = pick(record, range_probe)
    probe_a, probe_b = probe_ends(edge)
    row_a, row_b = swaps(row_a, row_b, "chan")
    fir = far(fir_taps)
    filtered, ends, lead, band, last_band = prepare(corange_probe, fir, space_taps)
    other, mine, give, keep = partials(
        record, row_a, row_b, range_probe, probe_a, probe_b, filtered, ends, lead, band
    )
    other = lax.ppermute(other, "chan", [(i, i ^ 1) for i in range(n_chan)])
    sums = pair_sum(mine, other)
    parts = [sums[0]]
    for distance in range(1, n_chan // 2):
        pairs = [(i, i ^ (2 * distance)) for i in range(n_chan)]
        parts.append(lax.ppermute(sums[distance], "chan", pairs))
    main, edge = corange_sum(parts)
    got = range_exchange(give, keep, main)
    corange_sketch = corange_edges(main, *swaps(edge, edge, "tm"))
    range_sketch = range_sum(last_band, got)
    return (range_sketch, corange_sketch)


def solution(mesh):
    return jax.shard_map(
        on_device,
        mesh=mesh,
        in_specs=(P("chan", "tm"), P(), P(), P("tm", None), P("chan", None)),
        out_specs=(P(("chan", "tm"), None), P("chan", "tm")),
        check_vma=False,
    )
```

```python
import functools

import jax
import jax.numpy as jnp
from jax import lax
from jax.experimental import pallas as pl
from jax.experimental.pallas import tpu as pltpu
from jax.sharding import PartitionSpec as P

TAPS = 129
HALF = 64
CHTAPS = 9
EDGE = 8
CHUNKS = 5
F32 = jnp.float32
BF16 = jnp.bfloat16
NT = (((1,), (1,)), ((), ()))
VMEM_LIMIT = 24 << 20

whole = functools.partial(pl.BlockSpec, memory_space=pltpu.VMEM)
smem = functools.partial(pl.BlockSpec, memory_space=pltpu.SMEM)
anywhere = functools.partial(pl.BlockSpec, memory_space=pl.ANY)
params = pltpu.CompilerParams(vmem_limit_bytes=VMEM_LIMIT)


def near(value):
    return pltpu.with_memory_space_constraint(value, pltpu.VMEM)


def split(value):
    high = value.astype(BF16)
    return high, (value - high.astype(F32)).astype(BF16)


def diagonals(row, rows, lanes, shift):
    spread = jnp.broadcast_to(row, (rows, lanes))
    return pltpu.roll(spread, shift % lanes, 1, stride=1, stride_axis=0)


def far(value):
    return pltpu.with_memory_space_constraint(value, pltpu.HBM)


def quick():
    return pl.CostEstimate(flops=0, bytes_accessed=0, transcendentals=0)


def taps_row(fir):
    taps = fir[...].astype(F32).reshape(1, TAPS)
    return jnp.concatenate([taps, jnp.zeros((1, 512 - TAPS), F32)], axis=1)


def prepare_kernel(probe, fir, space, filtered, ends, lead, band, last_band, padded):
    channels, width = probe.shape
    taps = taps_row(fir)
    lead[...] = diagonals(taps, 256, 512, -128)[:, :128].T.astype(BF16)
    late = pltpu.roll(jnp.broadcast_to(taps, (8, 512)), HALF, 1)[:1]
    band[...] = diagonals(late, 256, 512, 0).astype(BF16)
    lane = lax.broadcasted_iota(jnp.int32, (1, 256), 1)
    row = jnp.zeros((1, 256), F32)
    last_row = jnp.zeros((1, 256), F32)
    for tap in range(CHTAPS):
        row = jnp.where(lane == tap + 188, space[tap], row)
        last_row = jnp.where(lane == tap + 4, space[tap], last_row)
    last_band[...] = jnp.concatenate(list(split(diagonals(last_row[:, :128], 64, 128, 0))), axis=0)
    both = jnp.concatenate(list(split(diagonals(row, 256, 256, 0)[:, :128].T)), axis=0)
    padded[:192, :] = jnp.zeros((192, width), BF16)
    padded[192 + channels :, :] = jnp.zeros((192, width), BF16)
    padded[192 : 192 + channels, :] = probe[...]

    def block_of(block):
        pair = jnp.dot(both, padded[128 * block : 128 * block + 256, :], preferred_element_type=F32)
        return (pair[:128] + pair[128:]).T

    count = lax.axis_size("chan")
    chan = lax.axis_index("chan")
    share = width // count
    places = []
    for owner in range(count):
        here = lax.rem(chan, 2) == owner % 2
        place = lax.bitwise_xor(lax.div(chan, 2), owner // 2) + jnp.where(here, count // 2, 0)
        places.append(pl.multiple_of(place * share, share))

    def put(target, columns, value):
        for owner, place in enumerate(places):
            target[pl.ds(place, share), columns] = value[owner * share : (owner + 1) * share, :]

    last = channels // 128 + 1
    for block in range(1, last):
        put(filtered, slice(128 * block - 128, 128 * block), block_of(block).astype(BF16))
    lanes = lax.broadcasted_iota(jnp.int32, (width, 128), 1)
    put(ends, slice(0, 128), jnp.where(lanes < 64, block_of(last), block_of(0)).astype(BF16))


def prepare(probe, fir, space):
    channels, width = probe.shape
    return pl.pallas_call(
        prepare_kernel,
        in_specs=[whole(), whole(), smem()],
        out_specs=[whole()] * 5,
        out_shape=[
            pltpu.VMEM((width, channels), BF16),
            pltpu.VMEM((width, 128), BF16),
            pltpu.VMEM((128, 256), BF16),
            pltpu.VMEM((256, 512), BF16),
            pltpu.VMEM((128, 128), BF16),
        ],
        scratch_shapes=[
            pltpu.VMEM((channels + 384, width), BF16),
        ],
        compiler_params=params,
        cost_estimate=pl.CostEstimate(flops=0, bytes_accessed=8 << 20, transcendentals=0),
        name="prepare",
    )(near(probe), fir, far(space))


def range_part(give, keep, record, row_a, row_b, probe, probe_a, probe_b, lead, padded, probes, total):
    channels, samples = record.shape
    width = probe.shape[1]
    tm, chan = lax.axis_index("tm"), lax.axis_index("chan")
    count = lax.axis_size("tm")
    odd = lax.rem(chan, 2)
    padded[HALF : HALF + samples, :] = probe[...]
    padded[pl.ds(pl.multiple_of(odd * (HALF + samples), HALF), HALF), :] = probe_a[...]
    padded[pl.ds(pl.multiple_of((1 - odd) * (HALF + samples), HALF), HALF), :] = probe_b[...]
    for block in range(samples // 128):
        high, low = split(
            jnp.dot(lead[...], padded[128 * block : 128 * block + 256, :], preferred_element_type=F32)
        )
        probes[128 * block : 128 * block + 128, :width] = high
        probes[128 * block : 128 * block + 128, width:] = low
    edges = jnp.concatenate([row_a[...], row_b[...]], axis=0)
    pair = jnp.dot(edges, probes[...], preferred_element_type=F32)
    sums = pair[:, :width] + pair[:, width:]
    total[pl.ds(pl.multiple_of((1 - odd) * (EDGE + channels), EDGE), EDGE), :] = sums[:EDGE]
    total[pl.ds(pl.multiple_of(odd * (EDGE + channels), EDGE), EDGE), :] = sums[EDGE:]
    rows = channels // CHUNKS
    for start in range(0, channels, rows):
        pair = jnp.dot(record[start : start + rows, :], probes[...], preferred_element_type=F32)
        total[EDGE + start : EDGE + start + rows, :] = pair[:, :width] + pair[:, width:]

    share = channels // count
    for target, first in ((give, lax.bitwise_xor(tm, 1)), (keep, tm)):
        for index in range(count // 2):
            start = pl.multiple_of(lax.bitwise_xor(first, 2 * index) * share, EDGE)
            target[index] = total[pl.ds(start, share + 2 * EDGE), :].astype(target.dtype)


def corange_part(other, mine, record, row_a, row_b, filtered, ends, band, rim, pairs):
    channels, samples = record.shape
    width = filtered.shape[0]
    count = lax.axis_size("chan")
    chan = lax.axis_index("chan")
    odd = lax.rem(chan, 2)
    rim[...] = jnp.zeros_like(rim)
    rim[pl.ds(pl.multiple_of(odd * (128 - EDGE), EDGE), EDGE), :] = row_a[...].astype(F32)
    rim[pl.ds(pl.multiple_of((1 - odd) * (128 - EDGE), EDGE), EDGE), :] = row_b[...].astype(F32)
    pairs[:, :128] = jnp.zeros((2 * width, 128), BF16)
    pairs[:, 128 + samples :] = jnp.zeros((2 * width, 128), BF16)
    for block in range(0, samples, 512):
        value = jnp.dot(filtered[...], record[:, block : block + 512], preferred_element_type=F32)
        value = value + jnp.dot(
            ends[...], rim[:, block : block + 512].astype(BF16), preferred_element_type=F32
        )
        high, low = split(value)
        pairs[:width, 128 + block : 640 + block] = high
        pairs[width:, 128 + block : 640 + block] = low
    share = width // count

    def leave(columns, value):
        for index in range(count // 2):
            other[index, :, columns] = value[index * share : (index + 1) * share].astype(BF16)
            start = width // 2 + index * share
            mine[index, :, columns] = value[start : start + share]

    for block in range(0, samples, 256):
        pair = lax.dot_general(
            pairs[:, block : block + 512], band[...], NT, preferred_element_type=F32
        )
        leave(slice(block, block + 256), pair[:width] + pair[width:])
    pair = lax.dot_general(pairs[:, 128:256], band[:128, 256:384], NT, preferred_element_type=F32)
    pair = pair + lax.dot_general(
        pairs[:, samples : 128 + samples], band[:128, :128], NT, preferred_element_type=F32
    )
    leave(slice(samples, samples + 128), pair[:width] + pair[width:])


def partials_kernel(
    record, row_a, row_b, range_probe, probe_a, probe_b, filtered, ends, lead, band, other, mine, give, keep, *scratch
):
    range_part(give, keep, record, row_a, row_b, range_probe, probe_a, probe_b, lead, *scratch[:3])
    corange_part(other, mine, record, row_a, row_b, filtered, ends, band, *scratch[3:])


def partials(record, row_a, row_b, range_probe, probe_a, probe_b, filtered, ends, lead, band):
    n_tm, n_chan = lax.axis_size("tm"), lax.axis_size("chan")
    channels, samples = record.shape
    sketch, corange = range_probe.shape[1], filtered.shape[0]
    shape = (n_chan // 2, corange // n_chan, samples + 128)
    shares = (n_tm // 2, channels // n_tm + 2 * EDGE, sketch)
    return pl.pallas_call(
        partials_kernel,
        in_specs=[whole()] * 10,
        out_specs=[whole()] * 4,
        out_shape=[
            pltpu.VMEM(shape, BF16),
            pltpu.VMEM(shape, F32),
            pltpu.VMEM(shares, BF16),
            pltpu.VMEM(shares, F32),
        ],
        scratch_shapes=[
            pltpu.VMEM((samples + 2 * HALF, sketch), BF16),
            pltpu.VMEM((samples, 2 * sketch), BF16),
            pltpu.VMEM((channels + 2 * EDGE, sketch), F32),
            pltpu.VMEM((128, samples), F32),
            pltpu.VMEM((2 * corange, samples + 256), BF16),
        ],
        compiler_params=params,
        cost_estimate=quick(),
        name="partials",
    )(
        near(record), near(row_a), near(row_b), near(range_probe), near(probe_a), near(probe_b),
        filtered, ends, lead, band,
    )


def halve_kernel(held, got, after, give, keep):
    for index in range(keep.shape[0]):
        keep[index] = held[2 * index] + got[2 * index].astype(F32)
        give[index] = (held[2 * index + 1] + got[2 * index + 1].astype(F32)).astype(BF16)


def halve(held, got, after):
    shape = (held.shape[0] // 2, *held.shape[1:])
    return pl.pallas_call(
        halve_kernel,
        in_specs=[whole()] * 2 + [anywhere()],
        out_specs=[whole()] * 2,
        out_shape=[pltpu.VMEM(shape, BF16), pltpu.VMEM(shape, F32)],
        compiler_params=params,
        cost_estimate=quick(),
        name="halve",
    )(held, near(got), after)


def range_exchange(give, keep, after):
    count, distance = lax.axis_size("tm"), 1
    while True:
        got = lax.ppermute(give, "tm", [(i, i ^ distance) for i in range(count)])
        distance *= 2
        if distance == count:
            return keep, got
        give, keep = halve(keep, got, after)


def pair_sum_kernel(mine, got, *outs):
    for distance, out in enumerate(outs):
        out[...] = (mine[distance] + got[distance].astype(F32)).astype(out.dtype)


def pair_sum(mine, got):
    count, share, length = mine.shape
    return pl.pallas_call(
        pair_sum_kernel,
        in_specs=[whole()] * 2,
        out_specs=[whole()] * count,
        out_shape=[
            pltpu.VMEM((share, length), F32 if distance == 0 else BF16) for distance in range(count)
        ],
        compiler_params=params,
        cost_estimate=quick(),
        name="pair_sum",
    )(mine, near(got))


def corange_sum_kernel(*refs):
    parts, main, edge = refs[:-2], refs[-2], refs[-1]
    samples = main.shape[1]
    value = parts[0][...]
    for part in parts[1:]:
        value = value + part[...].astype(F32)
    main[...] = value[:, :samples]
    edge[...] = value[:, samples:]


def corange_sum(parts):
    share, length = parts[0].shape
    return pl.pallas_call(
        corange_sum_kernel,
        in_specs=[whole()] * len(parts),
        out_specs=[whole()] * 2,
        out_shape=[
            pltpu.VMEM((share, length - 128), F32),
            pltpu.VMEM((share, 128), F32),
        ],
        compiler_params=params,
        cost_estimate=quick(),
        name="corange_sum",
    )(*[near(part) for part in parts])


def corange_edges_kernel(main, edge_a, edge_b, out):
    odd = lax.rem(lax.axis_index("tm"), 2)
    samples = main.shape[1]
    lane = lax.broadcasted_iota(jnp.int32, edge_a.shape, 1)
    before = jnp.where(odd == 1, edge_a[...], edge_b[...])
    after = jnp.where(odd == 1, edge_b[...], edge_a[...])
    out[...] = main[...]
    out[:, :128] = main[:, :128] + jnp.where(lane < HALF, before, 0.0)
    out[:, samples - 128 :] = main[:, samples - 128 :] + jnp.where(lane >= HALF, after, 0.0)


def corange_edges(main, edge_a, edge_b):
    return pl.pallas_call(
        corange_edges_kernel,
        in_specs=[whole()] * 3,
        out_specs=whole(),
        out_shape=jax.ShapeDtypeStruct(main.shape, F32),
        compiler_params=params,
        cost_estimate=quick(),
        name="corange_edges",
    )(main, near(edge_a), near(edge_b))


def range_sum_kernel(band, *refs):
    parts, out, total = refs[:-2], refs[-2], refs[-1]
    value = parts[0][0] + parts[1][0].astype(F32)
    rows, width = value.shape
    high, low = split(value)
    total[:rows, :width] = high
    total[:rows, width:] = low
    total[rows:, :] = jnp.zeros((total.shape[0] - rows, 2 * width), BF16)
    for start in range(0, out.shape[0], 64):
        pair = jnp.dot(band[...], total[start : start + 128, :], preferred_element_type=F32)
        pair = pair[:64] + pair[64:]
        out[start : start + 64, :] = pair[:, :width] + pair[:, width:]


def range_sum(band, parts):
    _, rows, width = parts[0].shape
    return pl.pallas_call(
        range_sum_kernel,
        in_specs=[whole()] * (1 + len(parts)),
        out_specs=whole(),
        out_shape=jax.ShapeDtypeStruct((rows - 2 * EDGE, width), F32),
        scratch_shapes=[pltpu.VMEM((rows - 2 * EDGE + 64, 2 * width), BF16)],
        compiler_params=params,
        cost_estimate=quick(),
        name="range_sum",
    )(band, *[near(part) for part in parts])


def swaps(first, second, axis):
    count = lax.axis_size(axis)
    low = [(i, i ^ 1) for i in range(count)]
    high = [(i, i + 1) for i in range(1, count - 1, 2)]
    high = high + [(target, source) for source, target in high]
    return lax.ppermute(first, axis, low), lax.ppermute(second, axis, high)


def pick_kernel(record, probe, row_a, row_b, probe_a, sems):
    odd = lax.rem(lax.axis_index("chan"), 2)
    far_row, far_probe = record.shape[0] - EDGE, probe.shape[0] - HALF
    copies = [
        pltpu.make_async_copy(source.at[pl.ds(pl.multiple_of(start, size), size)], target, sems.at[slot])
        for slot, (source, start, size, target) in enumerate(
            [
                (record, (1 - odd) * far_row, EDGE, row_a),
                (record, odd * far_row, EDGE, row_b),
                (probe, (1 - odd) * far_probe, HALF, probe_a),
            ]
        )
    ]
    for copy in copies:
        copy.start()
    for copy in copies:
        copy.wait()


def pick(record, probe):
    rows = pltpu.VMEM((EDGE, record.shape[1]), BF16)
    return pl.pallas_call(
        pick_kernel,
        in_specs=[anywhere()] * 2,
        out_specs=[whole()] * 3,
        out_shape=[rows, rows, pltpu.VMEM((HALF, probe.shape[1]), BF16)],
        scratch_shapes=[pltpu.SemaphoreType.DMA((3,))],
        compiler_params=params,
        cost_estimate=pl.CostEstimate(flops=0, bytes_accessed=4 * record.size, transcendentals=0),
        name="pick",
    )(far(record), far(probe))


def probe_ends(edge):
    n_tm, n_chan = lax.axis_size("tm"), lax.axis_size("chan")
    pairs = []
    for chan in range(n_chan):
        for tm in range(n_tm - 1):
            low, high = chan * n_tm + tm, chan * n_tm + tm + 1
            pairs.append((low, high) if chan % 2 == 0 else (high, low))
    got = lax.ppermute(edge, ("chan", "tm"), pairs)
    return got, lax.ppermute(got, "chan", [(i, i ^ 1) for i in range(n_chan)])


def on_device(record, fir_taps, space_taps, range_probe, corange_probe):
    n_chan = lax.axis_size("chan")
    row_a, row_b, edge = pick(record, range_probe)
    probe_a, probe_b = probe_ends(edge)
    row_a, row_b = swaps(row_a, row_b, "chan")
    fir = far(fir_taps)
    filtered, ends, lead, band, last_band = prepare(corange_probe, fir, space_taps)
    other, mine, give, keep = partials(
        record, row_a, row_b, range_probe, probe_a, probe_b, filtered, ends, lead, band
    )
    other = lax.ppermute(other, "chan", [(i, i ^ 1) for i in range(n_chan)])
    sums = pair_sum(mine, other)
    parts = [sums[0]]
    for distance in range(n_chan // 2 - 1, 0, -1):
        pairs = [(i, i ^ (2 * distance)) for i in range(n_chan)]
        parts.append(lax.ppermute(sums[distance], "chan", pairs))
    main, edge = corange_sum(parts)
    got = range_exchange(give, keep, main)
    corange_sketch = corange_edges(main, *swaps(edge, edge, "tm"))
    range_sketch = range_sum(last_band, got)
    return (range_sketch, corange_sketch)


def solution(mesh):
    return jax.shard_map(
        on_device,
        mesh=mesh,
        in_specs=(P("chan", "tm"), P(), P(), P("tm", None), P("chan", None)),
        out_specs=(P(("chan", "tm"), None), P("chan", "tm")),
        check_vma=False,
    )
```

```python
import functools

import jax
import jax.numpy as jnp
from jax import lax
from jax.experimental import pallas as pl
from jax.experimental.pallas import tpu as pltpu
from jax.sharding import PartitionSpec as P

TAPS = 129
HALF = 64
CHTAPS = 9
EDGE = 8
CHUNKS = 5
F32 = jnp.float32
BF16 = jnp.bfloat16
NT = (((1,), (1,)), ((), ()))
VMEM_LIMIT = 24 << 20

whole = functools.partial(pl.BlockSpec, memory_space=pltpu.VMEM)
smem = functools.partial(pl.BlockSpec, memory_space=pltpu.SMEM)
anywhere = functools.partial(pl.BlockSpec, memory_space=pl.ANY)
params = pltpu.CompilerParams(vmem_limit_bytes=VMEM_LIMIT)


def near(value):
    return pltpu.with_memory_space_constraint(value, pltpu.VMEM)


def split(value):
    high = value.astype(BF16)
    return high, (value - high.astype(F32)).astype(BF16)


def diagonals(row, rows, lanes, shift):
    spread = jnp.broadcast_to(row, (rows, lanes))
    return pltpu.roll(spread, shift % lanes, 1, stride=1, stride_axis=0)


def far(value):
    return pltpu.with_memory_space_constraint(value, pltpu.HBM)


def quick():
    return pl.CostEstimate(flops=0, bytes_accessed=0, transcendentals=0)


def taps_row(fir):
    taps = fir[...].astype(F32).reshape(1, TAPS)
    return jnp.concatenate([taps, jnp.zeros((1, 512 - TAPS), F32)], axis=1)


def prepare_kernel(probe, fir, space, filtered, ends, lead, band, last_band, padded):
    channels, width = probe.shape
    taps = taps_row(fir)
    lead[...] = diagonals(taps, 256, 512, -128)[:, :128].T.astype(BF16)
    late = pltpu.roll(jnp.broadcast_to(taps, (8, 512)), HALF, 1)[:1]
    band[...] = diagonals(late, 256, 512, 0).astype(BF16)
    lane = lax.broadcasted_iota(jnp.int32, (1, 256), 1)
    row = jnp.zeros((1, 256), F32)
    last_row = jnp.zeros((1, 256), F32)
    for tap in range(CHTAPS):
        row = jnp.where(lane == tap + 188, space[tap], row)
        last_row = jnp.where(lane == tap + 4, space[tap], last_row)
    last_band[...] = jnp.concatenate(list(split(diagonals(last_row[:, :128], 64, 128, 0))), axis=0)
    both = jnp.concatenate(list(split(diagonals(row, 256, 256, 0)[:, :128].T)), axis=0)
    padded[:192, :] = jnp.zeros((192, width), BF16)
    padded[192 + channels :, :] = jnp.zeros((192, width), BF16)
    padded[192 : 192 + channels, :] = probe[...]

    def block_of(block):
        pair = jnp.dot(both, padded[128 * block : 128 * block + 256, :], preferred_element_type=F32)
        return (pair[:128] + pair[128:]).T

    count = lax.axis_size("chan")
    chan = lax.axis_index("chan")
    share = width // count
    places = []
    for owner in range(count):
        here = lax.rem(chan, 2) == owner % 2
        place = lax.bitwise_xor(lax.div(chan, 2), owner // 2) + jnp.where(here, count // 2, 0)
        places.append(pl.multiple_of(place * share, share))

    def put(target, columns, value):
        for owner, place in enumerate(places):
            target[pl.ds(place, share), columns] = value[owner * share : (owner + 1) * share, :]

    last = channels // 128 + 1
    for block in range(1, last):
        put(filtered, slice(128 * block - 128, 128 * block), block_of(block).astype(BF16))
    lanes = lax.broadcasted_iota(jnp.int32, (width, 128), 1)
    odd = lax.rem(chan, 2) == 1
    after, before = block_of(last), pltpu.roll(block_of(0), EDGE, 1)
    first = jnp.where(odd, before, after)
    second = pltpu.roll(jnp.where(odd, after, before), EDGE, 1)
    put(ends, slice(0, 128), jnp.where(lanes < EDGE, first, second).astype(BF16))


def prepare(probe, fir, space):
    channels, width = probe.shape
    return pl.pallas_call(
        prepare_kernel,
        in_specs=[whole(), whole(), smem()],
        out_specs=[whole()] * 5,
        out_shape=[
            pltpu.VMEM((width, channels), BF16),
            pltpu.VMEM((width, 128), BF16),
            pltpu.VMEM((128, 256), BF16),
            pltpu.VMEM((256, 512), BF16),
            pltpu.VMEM((128, 128), BF16),
        ],
        scratch_shapes=[
            pltpu.VMEM((channels + 384, width), BF16),
        ],
        compiler_params=params,
        cost_estimate=pl.CostEstimate(flops=0, bytes_accessed=8 << 20, transcendentals=0),
        name="prepare",
    )(near(probe), fir, far(space))


def range_part(give, keep, record, row_a, row_b, probe, probe_a, probe_b, lead, padded, probes, total):
    channels, samples = record.shape
    width = probe.shape[1]
    tm, chan = lax.axis_index("tm"), lax.axis_index("chan")
    count = lax.axis_size("tm")
    odd = lax.rem(chan, 2)
    padded[HALF : HALF + samples, :] = probe[...]
    padded[pl.ds(pl.multiple_of(odd * (HALF + samples), HALF), HALF), :] = probe_a[...]
    padded[pl.ds(pl.multiple_of((1 - odd) * (HALF + samples), HALF), HALF), :] = probe_b[...]
    for block in range(samples // 128):
        high, low = split(
            jnp.dot(lead[...], padded[128 * block : 128 * block + 256, :], preferred_element_type=F32)
        )
        probes[128 * block : 128 * block + 128, :width] = high
        probes[128 * block : 128 * block + 128, width:] = low
    edges = jnp.concatenate([row_a[...], row_b[...]], axis=0)
    pair = jnp.dot(edges, probes[...], preferred_element_type=F32)
    sums = pair[:, :width] + pair[:, width:]
    total[pl.ds(pl.multiple_of((1 - odd) * (EDGE + channels), EDGE), EDGE), :] = sums[:EDGE]
    total[pl.ds(pl.multiple_of(odd * (EDGE + channels), EDGE), EDGE), :] = sums[EDGE:]
    rows = channels // CHUNKS
    for start in range(0, channels, rows):
        pair = jnp.dot(record[start : start + rows, :], probes[...], preferred_element_type=F32)
        total[EDGE + start : EDGE + start + rows, :] = pair[:, :width] + pair[:, width:]

    share = channels // count
    for target, first in ((give, lax.bitwise_xor(tm, 1)), (keep, tm)):
        for index in range(count // 2):
            start = pl.multiple_of(lax.bitwise_xor(first, 2 * index) * share, EDGE)
            target[index] = total[pl.ds(start, share + 2 * EDGE), :].astype(target.dtype)


def corange_part(other, mine, record, row_a, row_b, filtered, ends, band, pairs):
    channels, samples = record.shape
    width = filtered.shape[0]
    count = lax.axis_size("chan")
    edges = jnp.concatenate([row_a[...], row_b[...]], axis=0)
    pairs[:, :128] = jnp.zeros((2 * width, 128), BF16)
    pairs[:, 128 + samples :] = jnp.zeros((2 * width, 128), BF16)
    for block in range(0, samples, 512):
        value = jnp.dot(filtered[...], record[:, block : block + 512], preferred_element_type=F32)
        value = value + jnp.dot(
            ends[:, : 2 * EDGE], edges[:, block : block + 512], preferred_element_type=F32
        )
        high, low = split(value)
        pairs[:width, 128 + block : 640 + block] = high
        pairs[width:, 128 + block : 640 + block] = low
    share = width // count

    def leave(columns, value):
        for index in range(count // 2):
            other[index, :, columns] = value[index * share : (index + 1) * share].astype(BF16)
            start = width // 2 + index * share
            mine[index, :, columns] = value[start : start + share]

    for block in range(0, samples, 256):
        pair = lax.dot_general(
            pairs[:, block : block + 512], band[...], NT, preferred_element_type=F32
        )
        leave(slice(block, block + 256), pair[:width] + pair[width:])
    pair = lax.dot_general(pairs[:, 128:256], band[:128, 256:384], NT, preferred_element_type=F32)
    pair = pair + lax.dot_general(
        pairs[:, samples : 128 + samples], band[:128, :128], NT, preferred_element_type=F32
    )
    leave(slice(samples, samples + 128), pair[:width] + pair[width:])


def partials_kernel(
    record, row_a, row_b, range_probe, probe_a, probe_b, filtered, ends, lead, band, other, mine, give, keep, *scratch
):
    range_part(give, keep, record, row_a, row_b, range_probe, probe_a, probe_b, lead, *scratch[:3])
    corange_part(other, mine, record, row_a, row_b, filtered, ends, band, *scratch[3:])


def partials(record, row_a, row_b, range_probe, probe_a, probe_b, filtered, ends, lead, band):
    n_tm, n_chan = lax.axis_size("tm"), lax.axis_size("chan")
    channels, samples = record.shape
    sketch, corange = range_probe.shape[1], filtered.shape[0]
    shape = (n_chan // 2, corange // n_chan, samples + 128)
    shares = (n_tm // 2, channels // n_tm + 2 * EDGE, sketch)
    return pl.pallas_call(
        partials_kernel,
        in_specs=[whole()] * 10,
        out_specs=[whole()] * 4,
        out_shape=[
            pltpu.VMEM(shape, BF16),
            pltpu.VMEM(shape, F32),
            pltpu.VMEM(shares, BF16),
            pltpu.VMEM(shares, F32),
        ],
        scratch_shapes=[
            pltpu.VMEM((samples + 2 * HALF, sketch), BF16),
            pltpu.VMEM((samples, 2 * sketch), BF16),
            pltpu.VMEM((channels + 2 * EDGE, sketch), F32),
            pltpu.VMEM((2 * corange, samples + 256), BF16),
        ],
        compiler_params=params,
        cost_estimate=quick(),
        name="partials",
    )(
        near(record), near(row_a), near(row_b), near(range_probe), near(probe_a), near(probe_b),
        filtered, ends, lead, band,
    )


def halve_kernel(held, got, after, give, keep):
    for index in range(keep.shape[0]):
        keep[index] = held[2 * index] + got[2 * index].astype(F32)
        give[index] = (held[2 * index + 1] + got[2 * index + 1].astype(F32)).astype(BF16)


def halve(held, got, after):
    shape = (held.shape[0] // 2, *held.shape[1:])
    return pl.pallas_call(
        halve_kernel,
        in_specs=[whole()] * 2 + [anywhere()],
        out_specs=[whole()] * 2,
        out_shape=[pltpu.VMEM(shape, BF16), pltpu.VMEM(shape, F32)],
        compiler_params=params,
        cost_estimate=quick(),
        name="halve",
    )(held, near(got), after)


def range_exchange(give, keep, after):
    count, distance = lax.axis_size("tm"), 1
    while True:
        got = lax.ppermute(give, "tm", [(i, i ^ distance) for i in range(count)])
        distance *= 2
        if distance == count:
            return keep, got
        give, keep = halve(keep, got, after)


def pair_sum_kernel(mine, got, *outs):
    for distance, out in enumerate(outs):
        out[...] = (mine[distance] + got[distance].astype(F32)).astype(out.dtype)


def pair_sum(mine, got):
    count, share, length = mine.shape
    return pl.pallas_call(
        pair_sum_kernel,
        in_specs=[whole()] * 2,
        out_specs=[whole()] * count,
        out_shape=[
            pltpu.VMEM((share, length), F32 if distance == 0 else BF16) for distance in range(count)
        ],
        compiler_params=params,
        cost_estimate=quick(),
        name="pair_sum",
    )(mine, near(got))


def corange_sum_kernel(*refs):
    parts, main, edge = refs[:-2], refs[-2], refs[-1]
    samples = main.shape[1]
    value = parts[0][...]
    for part in parts[1:]:
        value = value + part[...].astype(F32)
    main[...] = value[:, :samples]
    edge[...] = value[:, samples:]


def corange_sum(parts):
    share, length = parts[0].shape
    return pl.pallas_call(
        corange_sum_kernel,
        in_specs=[whole()] * len(parts),
        out_specs=[whole()] * 2,
        out_shape=[
            pltpu.VMEM((share, length - 128), F32),
            pltpu.VMEM((share, 128), F32),
        ],
        compiler_params=params,
        cost_estimate=quick(),
        name="corange_sum",
    )(*[near(part) for part in parts])


def corange_edges_kernel(main, edge_a, edge_b, out):
    odd = lax.rem(lax.axis_index("tm"), 2)
    samples = main.shape[1]
    lane = lax.broadcasted_iota(jnp.int32, edge_a.shape, 1)
    before = jnp.where(odd == 1, edge_a[...], edge_b[...])
    after = jnp.where(odd == 1, edge_b[...], edge_a[...])
    out[...] = main[...]
    out[:, :128] = main[:, :128] + jnp.where(lane < HALF, before, 0.0)
    out[:, samples - 128 :] = main[:, samples - 128 :] + jnp.where(lane >= HALF, after, 0.0)


def corange_edges(main, edge_a, edge_b):
    return pl.pallas_call(
        corange_edges_kernel,
        in_specs=[whole()] * 3,
        out_specs=whole(),
        out_shape=jax.ShapeDtypeStruct(main.shape, F32),
        compiler_params=params,
        cost_estimate=quick(),
        name="corange_edges",
    )(main, near(edge_a), near(edge_b))


def range_sum_kernel(band, *refs):
    parts, out, total = refs[:-2], refs[-2], refs[-1]
    value = parts[0][0] + parts[1][0].astype(F32)
    rows, width = value.shape
    high, low = split(value)
    total[:rows, :width] = high
    total[:rows, width:] = low
    total[rows:, :] = jnp.zeros((total.shape[0] - rows, 2 * width), BF16)
    for start in range(0, out.shape[0], 64):
        pair = jnp.dot(band[...], total[start : start + 128, :], preferred_element_type=F32)
        pair = pair[:64] + pair[64:]
        out[start : start + 64, :] = pair[:, :width] + pair[:, width:]


def range_sum(band, parts):
    _, rows, width = parts[0].shape
    return pl.pallas_call(
        range_sum_kernel,
        in_specs=[whole()] * (1 + len(parts)),
        out_specs=whole(),
        out_shape=jax.ShapeDtypeStruct((rows - 2 * EDGE, width), F32),
        scratch_shapes=[pltpu.VMEM((rows - 2 * EDGE + 64, 2 * width), BF16)],
        compiler_params=params,
        cost_estimate=quick(),
        name="range_sum",
    )(band, *[near(part) for part in parts])


def swaps(first, second, axis):
    count = lax.axis_size(axis)
    low = [(i, i ^ 1) for i in range(count)]
    high = [(i, i + 1) for i in range(1, count - 1, 2)]
    high = high + [(target, source) for source, target in high]
    return lax.ppermute(first, axis, low), lax.ppermute(second, axis, high)


def pick_kernel(record, probe, row_a, row_b, probe_a, sems):
    odd = lax.rem(lax.axis_index("chan"), 2)
    far_row, far_probe = record.shape[0] - EDGE, probe.shape[0] - HALF
    copies = [
        pltpu.make_async_copy(source.at[pl.ds(pl.multiple_of(start, size), size)], target, sems.at[slot])
        for slot, (source, start, size, target) in enumerate(
            [
                (record, (1 - odd) * far_row, EDGE, row_a),
                (record, odd * far_row, EDGE, row_b),
                (probe, (1 - odd) * far_probe, HALF, probe_a),
            ]
        )
    ]
    for copy in copies:
        copy.start()
    for copy in copies:
        copy.wait()


def pick(record, probe):
    rows = pltpu.VMEM((EDGE, record.shape[1]), BF16)
    return pl.pallas_call(
        pick_kernel,
        in_specs=[anywhere()] * 2,
        out_specs=[whole()] * 3,
        out_shape=[rows, rows, pltpu.VMEM((HALF, probe.shape[1]), BF16)],
        scratch_shapes=[pltpu.SemaphoreType.DMA((3,))],
        compiler_params=params,
        cost_estimate=pl.CostEstimate(flops=0, bytes_accessed=4 * record.size, transcendentals=0),
        name="pick",
    )(far(record), far(probe))


def probe_ends(edge):
    n_tm, n_chan = lax.axis_size("tm"), lax.axis_size("chan")
    pairs = []
    for chan in range(n_chan):
        for tm in range(n_tm - 1):
            low, high = chan * n_tm + tm, chan * n_tm + tm + 1
            pairs.append((low, high) if chan % 2 == 0 else (high, low))
    got = lax.ppermute(edge, ("chan", "tm"), pairs)
    return got, lax.ppermute(got, "chan", [(i, i ^ 1) for i in range(n_chan)])


def on_device(record, fir_taps, space_taps, range_probe, corange_probe):
    n_chan = lax.axis_size("chan")
    row_a, row_b, edge = pick(record, range_probe)
    probe_a, probe_b = probe_ends(edge)
    row_a, row_b = swaps(row_a, row_b, "chan")
    fir = far(fir_taps)
    filtered, ends, lead, band, last_band = prepare(corange_probe, fir, space_taps)
    other, mine, give, keep = partials(
        record, row_a, row_b, range_probe, probe_a, probe_b, filtered, ends, lead, band
    )
    other = lax.ppermute(other, "chan", [(i, i ^ 1) for i in range(n_chan)])
    sums = pair_sum(mine, other)
    parts = [sums[0]]
    for distance in range(n_chan // 2 - 1, 0, -1):
        pairs = [(i, i ^ (2 * distance)) for i in range(n_chan)]
        parts.append(lax.ppermute(sums[distance], "chan", pairs))
    main, edge = corange_sum(parts)
    got = range_exchange(give, keep, main)
    corange_sketch = corange_edges(main, *swaps(edge, edge, "tm"))
    range_sketch = range_sum(last_band, got)
    return (range_sketch, corange_sketch)


def solution(mesh):
    return jax.shard_map(
        on_device,
        mesh=mesh,
        in_specs=(P("chan", "tm"), P(), P(), P("tm", None), P("chan", None)),
        out_specs=(P(("chan", "tm"), None), P("chan", "tm")),
        check_vma=False,
    )
```

```python
import functools

import jax
import jax.numpy as jnp
from jax import lax
from jax.experimental import pallas as pl
from jax.experimental.pallas import tpu as pltpu
from jax.sharding import PartitionSpec as P

TAPS = 129
HALF = 64
CHTAPS = 9
EDGE = 8
CHUNKS = 5
F32 = jnp.float32
BF16 = jnp.bfloat16
NT = (((1,), (1,)), ((), ()))
VMEM_LIMIT = 24 << 20

whole = functools.partial(pl.BlockSpec, memory_space=pltpu.VMEM)
smem = functools.partial(pl.BlockSpec, memory_space=pltpu.SMEM)
anywhere = functools.partial(pl.BlockSpec, memory_space=pl.ANY)
params = pltpu.CompilerParams(vmem_limit_bytes=VMEM_LIMIT)


def near(value):
    return pltpu.with_memory_space_constraint(value, pltpu.VMEM)


def split(value):
    high = value.astype(BF16)
    return high, (value - high.astype(F32)).astype(BF16)


def diagonals(row, rows, lanes, shift):
    spread = jnp.broadcast_to(row, (rows, lanes))
    return pltpu.roll(spread, shift % lanes, 1, stride=1, stride_axis=0)


def far(value):
    return pltpu.with_memory_space_constraint(value, pltpu.HBM)


def quick():
    return pl.CostEstimate(flops=0, bytes_accessed=0, transcendentals=0)


def taps_row(fir):
    taps = fir[...].astype(F32).reshape(1, TAPS)
    return jnp.concatenate([taps, jnp.zeros((1, 512 - TAPS), F32)], axis=1)


def prepare_kernel(probe, fir, space, filtered, ends, lead, band, last_band, padded):
    channels, width = probe.shape
    taps = taps_row(fir)
    lead[...] = diagonals(taps, 256, 512, -128)[:, :128].T.astype(BF16)
    late = pltpu.roll(jnp.broadcast_to(taps, (8, 512)), HALF, 1)[:1]
    band[...] = diagonals(late, 256, 512, 0).astype(BF16)
    lane = lax.broadcasted_iota(jnp.int32, (1, 256), 1)
    row = jnp.zeros((1, 256), F32)
    last_row = jnp.zeros((1, 256), F32)
    for tap in range(CHTAPS):
        row = jnp.where(lane == tap + 188, space[tap], row)
        last_row = jnp.where(lane == tap + 4, space[tap], last_row)
    last_band[...] = jnp.concatenate(list(split(diagonals(last_row[:, :128], 64, 128, 0))), axis=0)
    both = jnp.concatenate(list(split(diagonals(row, 256, 256, 0)[:, :128].T)), axis=0)
    padded[:192, :] = jnp.zeros((192, width), BF16)
    padded[192 + channels :, :] = jnp.zeros((192, width), BF16)
    padded[192 : 192 + channels, :] = probe[...]

    def block_of(block):
        pair = jnp.dot(both, padded[128 * block : 128 * block + 256, :], preferred_element_type=F32)
        return (pair[:128] + pair[128:]).T

    count = lax.axis_size("chan")
    chan = lax.axis_index("chan")
    share = width // count
    places = []
    for owner in range(count):
        here = lax.rem(chan, 2) == owner % 2
        place = lax.bitwise_xor(lax.div(chan, 2), owner // 2) + jnp.where(here, count // 2, 0)
        places.append(pl.multiple_of(place * share, share))

    def put(target, columns, value):
        for owner, place in enumerate(places):
            target[pl.ds(place, share), columns] = value[owner * share : (owner + 1) * share, :]

    last = channels // 128 + 1
    for block in range(1, last):
        put(filtered, slice(128 * block - 128, 128 * block), block_of(block).astype(BF16))
    lanes = lax.broadcasted_iota(jnp.int32, (width, 128), 1)
    put(ends, slice(0, 128), jnp.where(lanes < 64, block_of(last), block_of(0)).astype(BF16))


def prepare(probe, fir, space):
    channels, width = probe.shape
    return pl.pallas_call(
        prepare_kernel,
        in_specs=[whole(), whole(), smem()],
        out_specs=[whole()] * 5,
        out_shape=[
            pltpu.VMEM((width, channels), BF16),
            pltpu.VMEM((width, 128), BF16),
            pltpu.VMEM((128, 256), BF16),
            pltpu.VMEM((256, 512), BF16),
            pltpu.VMEM((128, 128), BF16),
        ],
        scratch_shapes=[
            pltpu.VMEM((channels + 384, width), BF16),
        ],
        compiler_params=params,
        cost_estimate=pl.CostEstimate(flops=0, bytes_accessed=8 << 20, transcendentals=0),
        name="prepare",
    )(near(probe), fir, far(space))


def range_part(give, keep, record, row_a, row_b, probe, probe_a, probe_b, lead, padded, probes, total):
    channels, samples = record.shape
    width = probe.shape[1]
    tm, chan = lax.axis_index("tm"), lax.axis_index("chan")
    count = lax.axis_size("tm")
    odd = lax.rem(chan, 2)
    padded[HALF : HALF + samples, :] = probe[...]
    padded[pl.ds(pl.multiple_of(odd * (HALF + samples), HALF), HALF), :] = probe_a[...]
    padded[pl.ds(pl.multiple_of((1 - odd) * (HALF + samples), HALF), HALF), :] = probe_b[...]
    for block in range(samples // 128):
        high, low = split(
            jnp.dot(lead[...], padded[128 * block : 128 * block + 256, :], preferred_element_type=F32)
        )
        probes[128 * block : 128 * block + 128, :width] = high
        probes[128 * block : 128 * block + 128, width:] = low
    edges = jnp.concatenate([row_a[...], row_b[...]], axis=0)
    pair = jnp.dot(edges, probes[...], preferred_element_type=F32)
    sums = pair[:, :width] + pair[:, width:]
    total[pl.ds(pl.multiple_of((1 - odd) * (EDGE + channels), EDGE), EDGE), :] = sums[:EDGE]
    total[pl.ds(pl.multiple_of(odd * (EDGE + channels), EDGE), EDGE), :] = sums[EDGE:]
    rows = channels // CHUNKS
    for start in range(0, channels, rows):
        pair = jnp.dot(record[start : start + rows, :], probes[...], preferred_element_type=F32)
        total[EDGE + start : EDGE + start + rows, :] = pair[:, :width] + pair[:, width:]

    share = channels // count
    for target, first in ((give, lax.bitwise_xor(tm, 1)), (keep, tm)):
        for index in range(count // 2):
            start = pl.multiple_of(lax.bitwise_xor(first, 2 * index) * share, EDGE)
            target[index] = total[pl.ds(start, share + 2 * EDGE), :].astype(target.dtype)


def corange_part(other, mine, record, row_a, row_b, filtered, ends, band, rim, pairs):
    channels, samples = record.shape
    width = filtered.shape[0]
    count = lax.axis_size("chan")
    chan = lax.axis_index("chan")
    odd = lax.rem(chan, 2)
    rim[...] = jnp.zeros_like(rim)
    rim[pl.ds(pl.multiple_of(odd * (128 - EDGE), EDGE), EDGE), :] = row_a[...].astype(F32)
    rim[pl.ds(pl.multiple_of((1 - odd) * (128 - EDGE), EDGE), EDGE), :] = row_b[...].astype(F32)
    pairs[:, :128] = jnp.zeros((2 * width, 128), BF16)
    pairs[:, 128 + samples :] = jnp.zeros((2 * width, 128), BF16)
    for block in range(0, samples, 256):
        value = jnp.dot(filtered[...], record[:, block : block + 256], preferred_element_type=F32)
        value = value + jnp.dot(
            ends[...], rim[:, block : block + 256].astype(BF16), preferred_element_type=F32
        )
        high, low = split(value)
        pairs[:width, 128 + block : 384 + block] = high
        pairs[width:, 128 + block : 384 + block] = low
    share = width // count

    def leave(columns, value):
        for index in range(count // 2):
            other[index, :, columns] = value[index * share : (index + 1) * share].astype(BF16)
            start = width // 2 + index * share
            mine[index, :, columns] = value[start : start + share]

    for block in range(0, samples, 256):
        pair = lax.dot_general(
            pairs[:, block : block + 512], band[...], NT, preferred_element_type=F32
        )
        leave(slice(block, block + 256), pair[:width] + pair[width:])
    pair = lax.dot_general(pairs[:, 128:256], band[:128, 256:384], NT, preferred_element_type=F32)
    pair = pair + lax.dot_general(
        pairs[:, samples : 128 + samples], band[:128, :128], NT, preferred_element_type=F32
    )
    leave(slice(samples, samples + 128), pair[:width] + pair[width:])


def partials_kernel(
    record, row_a, row_b, range_probe, probe_a, probe_b, filtered, ends, lead, band, other, mine, give, keep, *scratch
):
    range_part(give, keep, record, row_a, row_b, range_probe, probe_a, probe_b, lead, *scratch[:3])
    corange_part(other, mine, record, row_a, row_b, filtered, ends, band, *scratch[3:])


def partials(record, row_a, row_b, range_probe, probe_a, probe_b, filtered, ends, lead, band):
    n_tm, n_chan = lax.axis_size("tm"), lax.axis_size("chan")
    channels, samples = record.shape
    sketch, corange = range_probe.shape[1], filtered.shape[0]
    shape = (n_chan // 2, corange // n_chan, samples + 128)
    shares = (n_tm // 2, channels // n_tm + 2 * EDGE, sketch)
    return pl.pallas_call(
        partials_kernel,
        in_specs=[whole()] * 10,
        out_specs=[whole()] * 4,
        out_shape=[
            pltpu.VMEM(shape, BF16),
            pltpu.VMEM(shape, F32),
            pltpu.VMEM(shares, BF16),
            pltpu.VMEM(shares, F32),
        ],
        scratch_shapes=[
            pltpu.VMEM((samples + 2 * HALF, sketch), BF16),
            pltpu.VMEM((samples, 2 * sketch), BF16),
            pltpu.VMEM((channels + 2 * EDGE, sketch), F32),
            pltpu.VMEM((128, samples), F32),
            pltpu.VMEM((2 * corange, samples + 256), BF16),
        ],
        compiler_params=params,
        cost_estimate=quick(),
        name="partials",
    )(
        near(record), near(row_a), near(row_b), near(range_probe), near(probe_a), near(probe_b),
        filtered, ends, lead, band,
    )


def halve_kernel(held, got, after, give, keep):
    for index in range(keep.shape[0]):
        keep[index] = held[2 * index] + got[2 * index].astype(F32)
        give[index] = (held[2 * index + 1] + got[2 * index + 1].astype(F32)).astype(BF16)


def halve(held, got, after):
    shape = (held.shape[0] // 2, *held.shape[1:])
    return pl.pallas_call(
        halve_kernel,
        in_specs=[whole()] * 2 + [anywhere()],
        out_specs=[whole()] * 2,
        out_shape=[pltpu.VMEM(shape, BF16), pltpu.VMEM(shape, F32)],
        compiler_params=params,
        cost_estimate=quick(),
        name="halve",
    )(held, near(got), after)


def range_exchange(give, keep, after):
    count, distance = lax.axis_size("tm"), 1
    while True:
        got = lax.ppermute(give, "tm", [(i, i ^ distance) for i in range(count)])
        distance *= 2
        if distance == count:
            return keep, got
        give, keep = halve(keep, got, after)


def pair_sum_kernel(mine, got, *outs):
    for distance, out in enumerate(outs):
        out[...] = (mine[distance] + got[distance].astype(F32)).astype(out.dtype)


def pair_sum(mine, got):
    count, share, length = mine.shape
    return pl.pallas_call(
        pair_sum_kernel,
        in_specs=[whole()] * 2,
        out_specs=[whole()] * count,
        out_shape=[
            pltpu.VMEM((share, length), F32 if distance == 0 else BF16) for distance in range(count)
        ],
        compiler_params=params,
        cost_estimate=quick(),
        name="pair_sum",
    )(mine, near(got))


def corange_sum_kernel(*refs):
    parts, main, edge = refs[:-2], refs[-2], refs[-1]
    samples = main.shape[1]
    value = parts[0][...]
    for part in parts[1:]:
        value = value + part[...].astype(F32)
    main[...] = value[:, :samples]
    edge[...] = value[:, samples:]


def corange_sum(parts):
    share, length = parts[0].shape
    return pl.pallas_call(
        corange_sum_kernel,
        in_specs=[whole()] * len(parts),
        out_specs=[whole()] * 2,
        out_shape=[
            pltpu.VMEM((share, length - 128), F32),
            pltpu.VMEM((share, 128), F32),
        ],
        compiler_params=params,
        cost_estimate=quick(),
        name="corange_sum",
    )(*[near(part) for part in parts])


def corange_edges_kernel(main, edge_a, edge_b, out):
    odd = lax.rem(lax.axis_index("tm"), 2)
    samples = main.shape[1]
    lane = lax.broadcasted_iota(jnp.int32, edge_a.shape, 1)
    before = jnp.where(odd == 1, edge_a[...], edge_b[...])
    after = jnp.where(odd == 1, edge_b[...], edge_a[...])
    out[...] = main[...]
    out[:, :128] = main[:, :128] + jnp.where(lane < HALF, before, 0.0)
    out[:, samples - 128 :] = main[:, samples - 128 :] + jnp.where(lane >= HALF, after, 0.0)


def corange_edges(main, edge_a, edge_b):
    return pl.pallas_call(
        corange_edges_kernel,
        in_specs=[whole()] * 3,
        out_specs=whole(),
        out_shape=jax.ShapeDtypeStruct(main.shape, F32),
        compiler_params=params,
        cost_estimate=quick(),
        name="corange_edges",
    )(main, near(edge_a), near(edge_b))


def range_sum_kernel(band, *refs):
    parts, out, total = refs[:-2], refs[-2], refs[-1]
    value = parts[0][0] + parts[1][0].astype(F32)
    rows, width = value.shape
    high, low = split(value)
    total[:rows, :width] = high
    total[:rows, width:] = low
    total[rows:, :] = jnp.zeros((total.shape[0] - rows, 2 * width), BF16)
    for start in range(0, out.shape[0], 64):
        pair = jnp.dot(band[...], total[start : start + 128, :], preferred_element_type=F32)
        pair = pair[:64] + pair[64:]
        out[start : start + 64, :] = pair[:, :width] + pair[:, width:]


def range_sum(band, parts):
    _, rows, width = parts[0].shape
    return pl.pallas_call(
        range_sum_kernel,
        in_specs=[whole()] * (1 + len(parts)),
        out_specs=whole(),
        out_shape=jax.ShapeDtypeStruct((rows - 2 * EDGE, width), F32),
        scratch_shapes=[pltpu.VMEM((rows - 2 * EDGE + 64, 2 * width), BF16)],
        compiler_params=params,
        cost_estimate=quick(),
        name="range_sum",
    )(band, *[near(part) for part in parts])


def swaps(first, second, axis):
    count = lax.axis_size(axis)
    low = [(i, i ^ 1) for i in range(count)]
    high = [(i, i + 1) for i in range(1, count - 1, 2)]
    high = high + [(target, source) for source, target in high]
    return lax.ppermute(first, axis, low), lax.ppermute(second, axis, high)


def pick_kernel(record, probe, row_a, row_b, probe_a, sems):
    odd = lax.rem(lax.axis_index("chan"), 2)
    far_row, far_probe = record.shape[0] - EDGE, probe.shape[0] - HALF
    copies = [
        pltpu.make_async_copy(source.at[pl.ds(pl.multiple_of(start, size), size)], target, sems.at[slot])
        for slot, (source, start, size, target) in enumerate(
            [
                (record, (1 - odd) * far_row, EDGE, row_a),
                (record, odd * far_row, EDGE, row_b),
                (probe, (1 - odd) * far_probe, HALF, probe_a),
            ]
        )
    ]
    for copy in copies:
        copy.start()
    for copy in copies:
        copy.wait()


def pick(record, probe):
    rows = pltpu.VMEM((EDGE, record.shape[1]), BF16)
    return pl.pallas_call(
        pick_kernel,
        in_specs=[anywhere()] * 2,
        out_specs=[whole()] * 3,
        out_shape=[rows, rows, pltpu.VMEM((HALF, probe.shape[1]), BF16)],
        scratch_shapes=[pltpu.SemaphoreType.DMA((3,))],
        compiler_params=params,
        cost_estimate=pl.CostEstimate(flops=0, bytes_accessed=4 * record.size, transcendentals=0),
        name="pick",
    )(far(record), far(probe))


def probe_ends(edge):
    n_tm, n_chan = lax.axis_size("tm"), lax.axis_size("chan")
    pairs = []
    for chan in range(n_chan):
        for tm in range(n_tm - 1):
            low, high = chan * n_tm + tm, chan * n_tm + tm + 1
            pairs.append((low, high) if chan % 2 == 0 else (high, low))
    got = lax.ppermute(edge, ("chan", "tm"), pairs)
    return got, lax.ppermute(got, "chan", [(i, i ^ 1) for i in range(n_chan)])


def on_device(record, fir_taps, space_taps, range_probe, corange_probe):
    n_chan = lax.axis_size("chan")
    row_a, row_b, edge = pick(record, range_probe)
    probe_a, probe_b = probe_ends(edge)
    row_a, row_b = swaps(row_a, row_b, "chan")
    fir = far(fir_taps)
    filtered, ends, lead, band, last_band = prepare(corange_probe, fir, space_taps)
    other, mine, give, keep = partials(
        record, row_a, row_b, range_probe, probe_a, probe_b, filtered, ends, lead, band
    )
    other = lax.ppermute(other, "chan", [(i, i ^ 1) for i in range(n_chan)])
    sums = pair_sum(mine, other)
    parts = [sums[0]]
    for distance in range(n_chan // 2 - 1, 0, -1):
        pairs = [(i, i ^ (2 * distance)) for i in range(n_chan)]
        parts.append(lax.ppermute(sums[distance], "chan", pairs))
    main, edge = corange_sum(parts)
    got = range_exchange(give, keep, main)
    corange_sketch = corange_edges(main, *swaps(edge, edge, "tm"))
    range_sketch = range_sum(last_band, got)
    return (range_sketch, corange_sketch)


def solution(mesh):
    return jax.shard_map(
        on_device,
        mesh=mesh,
        in_specs=(P("chan", "tm"), P(), P(), P("tm", None), P("chan", None)),
        out_specs=(P(("chan", "tm"), None), P("chan", "tm")),
        check_vma=False,
    )
```
